256 devices in a mesh: bricks: 256 (over z, y, x, core).
Axes of the slice: x: 4, y: 4, z: 8, core: 2. Of those that a mesh axis runs over, the one named last changes fastest.
Arguments:
- voxels: bfloat16 [1536, 64, 512], P('bricks'), may hold values from -6 to 6
- kernel: bfloat16 [64, 8, 3, 3, 3], replicated, may hold values from -0.4375 to 0.4375
- bias: float32 [64], replicated, may hold values from -3 to 3
- cortex: int32 [1536, 512], P('bricks'), may hold values 0 or 1
- slot_to_brick: int32 [1536], P('bricks'), may hold values from -1 to 767, as said below
- neighbors: int32 [1536, 6], P('bricks'), may hold values from -1 to 1535, as said below
- cotangent: bfloat16 [1536, 64, 512], P('bricks'), may hold values from -6 to 6
Outputs:
- activated: bfloat16 [1536, 64, 512], P('bricks')
- input_grad: bfloat16 [1536, 64, 512], P('bricks')
- kernel_grad: float32 [64, 8, 3, 3, 3], replicated
- bias_grad: float32 [64], replicated
The draws below stay inside these ranges and needn't reach their ends.
Inputs may be any that keep to these rules, and one draw needn't show every extreme that they name: `slot_to_brick`: the bricks 0 to 767 form a tube of 2 x 2 bricks in cross-section along the first dimension, brick (p, q, r) numbered (p 2 + q) 2 + r. Each device holds a run of consecutive bricks in its first slots, in order, the runs following device order; a device holds 2 to 6 bricks, some device exactly 6; its other slots hold -1. `neighbors`: the slot index of the brick across each face of the slot's brick in that tube, -1 outside the tube and for empty slots; the relation is symmetric. A brick across a face of the first dimension lies on a device at most 2 away, across the other faces at most 1 away, and both distances occur.
All inputs are finite; a program needn't handle non-finite values. No bound on the sum of `cortex` on one device may be relied on, other than what follows from the above.
Results may differ from the reference program's by a relative error of at most 0.0075.
Values may be sent and summed in bfloat16 or wider, within the bound.
A program may use at most 128 MiB of HBM per device.

```python
import jax
import jax.numpy as jnp
from jax import lax

CHANNEL_COUNT = 64
GROUPS = 8
GC = 8
E = 8
SLOTS = 6
BRICK_VOXELS = 512
TOTAL_SLOTS = 1536
NBRICK = 768
N_BRICKS = 256


def deal_bricks(key):
    base_key = jax.random.fold_in(key, 1234)
    group_count = N_BRICKS // 4
    kinds = jax.random.randint(jax.random.fold_in(base_key, 1), (group_count,), 0, 3)
    kinds = kinds.at[0].set(0)
    neighbor_patterns = jnp.array([[6, 2, 2, 2], [4, 4, 2, 2], [3, 3, 3, 3]], dtype=jnp.int32)
    chosen = neighbor_patterns[kinds]
    sub_keys = jax.random.split(jax.random.fold_in(base_key, 2), group_count)
    orders = jax.vmap(lambda sub_key: jax.random.permutation(sub_key, 4))(sub_keys)
    counts = jnp.take_along_axis(chosen, orders, axis=1).reshape(-1).astype(jnp.int32)
    starts = (jnp.cumsum(counts) - counts).astype(jnp.int32)
    positions = jnp.arange(SLOTS, dtype=jnp.int32)
    held = jnp.where(positions[None, :] < counts[:, None], starts[:, None] + positions[None, :], -1)
    return (held.reshape(-1).astype(jnp.int32), starts)


def draw_slot_to_brick(key, part):
    return deal_bricks(key)[0]


def draw_neighbors(key, part):
    held, starts = deal_bricks(key)
    tube_len = NBRICK // 4
    safe = jnp.maximum(held, 0)
    along = safe // 4
    second = safe // 2 % 2
    third = safe % 2
    candidate = jnp.stack([safe - 4, safe + 4, safe - 2, safe + 2, safe - 1, safe + 1], axis=1)
    valid = jnp.stack([along > 0, along < tube_len - 1, second == 1, second == 0, third == 1, third == 0], axis=1)
    valid = valid & (held >= 0)[:, None]
    target = jnp.where(valid, candidate, 0)
    owner = jnp.sum((starts[None, None, :] <= target[:, :, None]).astype(jnp.int32), axis=2) - 1
    slot_index = owner * SLOTS + target - starts[owner]
    return jnp.where(valid, slot_index, -1).astype(jnp.int32)


def plant(result, key, least, top_value):
    spot = [jax.random.randint(jax.random.fold_in(key, axis), (), 0, length) for axis, length in enumerate(result.shape)]
    main_axis = result.shape.index(max(result.shape))
    neighbour = spot[:main_axis] + [(spot[main_axis] + 1) % result.shape[main_axis]] + spot[main_axis + 1:]
    return result.at[tuple(spot)].set(least).at[tuple(neighbour)].set(top_value)


def shard_levels(key, dims, cuts, low, largest):
    level = 1.0
    for dim, blocks in cuts:
        heights = jax.random.uniform(jax.random.fold_in(jax.random.fold_in(key, 6), dim), (blocks,), jnp.float32, low / len(cuts), largest / len(cuts))
        level = level * jnp.repeat(jnp.exp(heights), dims[dim] // blocks).reshape((-1,) + (1,) * (len(dims) - 1 - dim))
    return level


def noise(key, dims, spread, limit, cuts=(), kind=jnp.bfloat16):
    values = jax.random.normal(key, dims, jnp.float32) * spread
    if len(cuts) > 0:
        values = shard_levels(key, dims, cuts, -0.22, 0.18) * values
    return jnp.clip(values, min=-limit, max=limit).astype(kind)


def setup_inputs(seed: int = 0) -> dict:
    arg_keys = jax.random.split(jax.random.key(seed), 8)
    voxels = noise(arg_keys[0], (TOTAL_SLOTS, CHANNEL_COUNT, BRICK_VOXELS), 1.0, 6.0, ((0, 256),))
    kernel = noise(arg_keys[1], (CHANNEL_COUNT, GC, 3, 3, 3), (GC * 27) ** -0.5, 0.4375)
    bias = noise(arg_keys[2], (CHANNEL_COUNT,), 0.5, 3.0, (), jnp.float32)
    cortex = plant((jax.random.randint(arg_keys[3], (TOTAL_SLOTS, BRICK_VOXELS), 0, 3) < 2).astype(jnp.int32), jax.random.fold_in(arg_keys[3], 1), 0, 1)
    slot_to_brick = draw_slot_to_brick(jax.random.fold_in(arg_keys[7], 71), 0)
    neighbors = draw_neighbors(jax.random.fold_in(arg_keys[7], 71), 0)
    cotangent = noise(arg_keys[6], (TOTAL_SLOTS, CHANNEL_COUNT, BRICK_VOXELS), 1.0, 6.0, ((0, 256),))
    return dict(voxels=voxels, kernel=kernel, bias=bias, cortex=cortex, slot_to_brick=slot_to_brick, neighbors=neighbors, cotangent=cotangent)


def follow(link_table, slot_index, facet_position):
    return jnp.where(slot_index >= 0, link_table[jnp.maximum(slot_index, 0), facet_position], -1)

def padded_brick(whole_field, link_table, slot_index):
    edge_len = whole_field.shape[2]
    chosen = {-1: slice(edge_len - 1, edge_len), 0: slice(0, edge_len), 1: slice(0, 1)}
    layers = []
    for step_x in (-1, 0, 1):
        columns = []
        for step_y in (-1, 0, 1):
            entries = []
            for step_z in (-1, 0, 1):
                target = slot_index
                if step_z != 0:
                    target = follow(link_table, target, 4 if step_z < 0 else 5)
                if step_y != 0:
                    target = follow(link_table, target, 2 if step_y < 0 else 3)
                if step_x != 0:
                    target = follow(link_table, target, 0 if step_x < 0 else 1)
                brick_data = whole_field[jnp.maximum(target, 0)]
                window = brick_data[:, chosen[step_x], chosen[step_y], chosen[step_z]]
                entries.append(jnp.where(target >= 0, window, jnp.zeros_like(window)))
            columns.append(jnp.concatenate(entries, axis=3))
        layers.append(jnp.concatenate(columns, axis=2))
    return jnp.concatenate(layers, axis=1)

def grouped(inputs, weights):
    return lax.conv_general_dilated(inputs, weights, (1, 1, 1), 'VALID', dimension_numbers=('NCDHW', 'OIDHW', 'NCDHW'), feature_group_count=GROUPS, precision=lax.Precision.HIGHEST)

def reference(voxels, kernel, bias, cortex, slot_to_brick, neighbors, cotangent):
    slot_count = voxels.shape[0]
    cube = (slot_count, CHANNEL_COUNT, E, E, E)
    fields = voxels.reshape(cube)
    upstream = cotangent.reshape(cube)
    occupied = (slot_to_brick >= 0).astype(jnp.int32)
    keeper = (cortex.reshape(slot_count, E, E, E) * occupied[:, None, None, None]).astype(jnp.float32)
    forward_weights = kernel.astype(jnp.float32)
    six_dim = forward_weights.reshape(GROUPS, GC, GC, 3, 3, 3)
    flipped = jnp.transpose(six_dim, (0, 2, 1, 3, 4, 5))[:, :, :, ::-1, ::-1, ::-1].reshape(CHANNEL_COUNT, GC, 3, 3, 3)
    indices = jnp.arange(slot_count, dtype=jnp.int32)

    def forward_slot(slot_index):
        padded = padded_brick(fields, neighbors, slot_index).astype(jnp.float32)
        pre = grouped(padded[None], forward_weights)[0] + bias[:, None, None, None]
        keep_slot = keeper[slot_index][None]
        sigma = jax.nn.sigmoid(pre)
        activated = (pre * sigma * keep_slot).astype(jnp.bfloat16)
        slope = sigma * (1.0 + pre * (1.0 - sigma))
        dpre = (upstream[slot_index].astype(jnp.float32) * keep_slot * slope).astype(jnp.bfloat16)
        return (activated, dpre)
    activated, dpre_all = lax.map(forward_slot, indices)

    def backward_slot(carry, slot_index):
        kernel_sum, bias_sum = carry
        padded = padded_brick(fields, neighbors, slot_index).astype(jnp.float32)
        grad_pad = padded_brick(dpre_all, neighbors, slot_index).astype(jnp.float32)
        input_grad = grouped(grad_pad[None], flipped)[0].astype(jnp.bfloat16)
        term = dpre_all[slot_index].astype(jnp.float32)
        output_bricks, pullback = jax.vjp(lambda weights_in: grouped(padded[None], weights_in), forward_weights)
        kernel_term = pullback(term[None])[0]
        return ((kernel_sum + kernel_term, bias_sum + lax.optimization_barrier(jnp.sum(term, axis=(1, 2, 3)))), input_grad)
    start = (jnp.zeros_like(forward_weights), jnp.zeros((CHANNEL_COUNT,), jnp.float32))
    totals, input_grad = lax.scan(backward_slot, start, indices)
    return (activated.reshape(slot_count, CHANNEL_COUNT, BRICK_VOXELS), input_grad.reshape(slot_count, CHANNEL_COUNT, BRICK_VOXELS), totals[0], totals[1])
```

```python
import functools

import jax
import jax.numpy as jnp
from jax import lax
from jax.experimental import pallas as pl
from jax.experimental.pallas import tpu as pltpu
from jax.sharding import PartitionSpec as P

AXIS = "bricks"
CH = 64
GC = 8
V = 512
SLOTS = 6
REACH = 4
WIN = 7
MSG_ROWS = (320, 144, 48, 16)
MSG_BASE = (0, 320, 464, 512)
MSG_TOTAL = 528
F32 = jnp.float32
BF16 = jnp.bfloat16
MESH = pl.DeviceIdType.MESH


def plane_size(devices):
    return 32 if devices >= 64 else devices // 2


def lanes(shape):
    return lax.broadcasted_iota(jnp.int32, shape, len(shape) - 1)


def low_half(shape):
    return lanes(shape) < CH


def swap_halves(value):
    return pltpu.roll(value, CH, value.ndim - 1)


def kernel_body(
    devices,
    planes,
    brick_ref,
    vox_ref,
    cot_ref,
    cortex_ref,
    taps_ref,
    bias_ref,
    act_ref,
    grad_ref,
    kg_ref,
    bg_ref,
    field,
    padded,
    weight_fwd,
    weight_bwd,
    xh,
    xl,
    yb,
    yf,
    zb,
    zf,
    eh,
    el,
    lh,
    ll,
    send1,
    recv1,
    send2,
    recv2,
    acc,
    bias_acc,
    part,
    scattered,
    stacked,
    final,
    ssem1,
    rsem1,
    ssem2,
    rsem2,
    ssem_a,
    rsem_a,
    ssem_b,
    rsem_b,
    ssem_c,
    rsem_c,
):
    plane = plane_size(devices)
    me = lax.axis_index(AXIS)
    mine = lax.rem(me, plane)
    level = me // plane

    def plane_peer(i):
        return level * plane + lax.rem(mine + i, plane)

    def level_peer(i):
        return lax.rem(level + i, planes) * plane + mine

    barrier = pltpu.get_barrier_semaphore()
    for k in range(1, REACH + 1):
        for sign in (-1, 1):
            pl.semaphore_signal(
                barrier,
                inc=1,
                device_id=(lax.rem(me + devices + sign * k, devices),),
                device_id_type=MESH,
            )

    @pl.loop(1, plane)
    def _(i):
        pl.semaphore_signal(barrier, inc=1, device_id=(plane_peer(i),), device_id_type=MESH)

    @pl.loop(1, planes)
    def _(i):
        pl.semaphore_signal(barrier, inc=1, device_id=(level_peer(i),), device_id_type=MESH)

    first = brick_ref[0]
    count = jnp.int32(0)
    for j in range(SLOTS):
        count = count + jnp.where(brick_ref[j] >= 0, 1, 0).astype(jnp.int32)

    def forward_index(m):
        return jnp.minimum(jnp.where(m < count, m, SLOTS + m - count), 12)

    row_group = lax.broadcasted_iota(jnp.int32, (CH, 128), 0) // GC
    col_group = lax.rem(lanes((CH, 128)), CH) // GC
    same_group = row_group == col_group
    left = low_half((CH, 128))
    zero_half = jnp.zeros((GC, CH), F32)

    def spread(first_tap, second_tap):
        one = taps_ref[first_tap].astype(F32)
        two = zero_half if second_tap is None else taps_ref[second_tap].astype(F32)
        both = jnp.concatenate([one, two], axis=1)
        return jnp.where(same_group, jnp.concatenate([both] * GC, axis=0), 0.0).astype(BF16)

    blank = jnp.zeros((CH, 256), BF16)
    for a in range(3):
        for c in range(3):
            rows = slice(c * CH, (c + 1) * CH)
            weight_fwd[a, rows, 0:128] = spread(a * 9 + c, a * 9 + 3 + c)
            weight_fwd[a, rows, 128:256] = spread(a * 9 + 6 + c, None)
        weight_fwd[a, 3 * CH : 4 * CH, :] = blank
        for b in range(3):
            rows = slice(b * CH, (b + 1) * CH)
            base = (2 - a) * 9 + (2 - b) * 3
            weight_bwd[a, rows, 0:128] = spread(base + 2, base + 1)
            weight_bwd[a, rows, 128:256] = spread(base, None)
        weight_bwd[a, 3 * CH : 4 * CH, :] = blank

    def slot_facts(j):
        brick = brick_ref[j]
        held = brick >= 0
        safe = jnp.maximum(brick, 0)
        return held, safe // 4, lax.rem(safe // 2, 2), lax.rem(safe, 2)

    def own_tables(j):
        held, _, q, r = slot_facts(j)
        q0, r0 = q == 0, r == 0
        high = field[j, 448:512, :]
        low = field[j, 0:64, :]
        xh[j + 4] = high
        xl[j] = low
        cube = field[j].reshape(8, 8, 8, 128)
        side = jnp.where(q0, cube[:, 7], cube[:, 0]).reshape(64, 128)
        yb[j + 2] = side
        yf[j] = side
        deep = jnp.where(
            r0, field[j, pl.ds(7, 64, stride=8), :], field[j, pl.ds(0, 64, stride=8), :]
        )
        zb[j + 1] = deep
        zf[j] = deep
        for table, at, start in ((eh, j + 7, 448), (el, j, 0)):
            table[at, 0:8, :] = jnp.where(
                q0, field[j, start + 56 : start + 64, :], field[j, start : start + 8, :]
            )
            table[at, 8:16, :] = jnp.where(
                r0,
                field[j, pl.ds(start + 7, 8, stride=8), :],
                field[j, pl.ds(start, 8, stride=8), :],
            )
        line = jnp.where(
            q0,
            jnp.where(
                r0,
                field[j, pl.ds(63, 8, stride=64), :],
                field[j, pl.ds(56, 8, stride=64), :],
            ),
            jnp.where(
                r0,
                field[j, pl.ds(7, 8, stride=64), :],
                field[j, pl.ds(0, 8, stride=64), :],
            ),
        )
        lh[j + 7] = line
        ll[j] = line

    def pack(send):
        half64 = low_half((64, 128))
        half32 = low_half((32, 128))
        half8 = low_half((8, 128))
        number = jnp.zeros((8, 128), F32) + count.astype(F32)
        for way in range(2):
            if way == 0:
                face, side, deep, edge, line = xh, yb, zb, eh, lh

                def at(table, j, ahead):
                    return table[ahead + jnp.maximum(count - j, 0)]

                shifts = (4, 2, 1, 7, 7)
            else:
                face, side, deep, edge, line = xl, yf, zf, el, ll

                def at(table, j, ahead):
                    return table[j - 1]

                shifts = (0, 0, 0, 0, 0)

            def pair(one, two):
                return jnp.where(half64, one, two).astype(BF16)

            f = [at(face, j, shifts[0]) for j in range(1, 5)]
            send[way, 0:64, :] = pair(f[0], f[1])
            send[way, 64:128, :] = pair(f[2], f[3])
            send[way, 128:192, :] = pair(at(side, 1, shifts[1]), at(side, 2, shifts[1]))
            d = at(deep, 1, shifts[2])
            send[way, 192:224, :] = jnp.where(half32, d[0:32], d[32:64]).astype(BF16)
            send[way, 320:384, :] = pair(f[0], f[1])
            for j in range(1, 7):
                e = at(edge, j, shifts[3])
                n = at(line, j, shifts[4])
                tile = jnp.concatenate(
                    [jnp.where(half8, e[0:8], n), jnp.where(half8, e[8:16], number)], axis=0
                ).astype(BF16)
                send[way, 224 + 16 * (j - 1) : 240 + 16 * (j - 1), :] = tile
                if j <= 5:
                    send[way, 384 + 16 * (j - 1) : 400 + 16 * (j - 1), :] = tile
                if j <= 3:
                    send[way, 464 + 16 * (j - 1) : 480 + 16 * (j - 1), :] = tile
                if j == 1:
                    send[way, 512:528, :] = tile

    def halo_copies(send, recv, ssem, rsem):
        copies = []
        for way, sign in ((0, 1), (1, -1)):
            for k in range(1, REACH + 1):
                rows = pl.ds(MSG_BASE[k - 1], MSG_ROWS[k - 1])
                copies.append(
                    pltpu.make_async_remote_copy(
                        src_ref=send.at[way, rows, :],
                        dst_ref=recv.at[way, rows, :],
                        send_sem=ssem.at[way, k - 1],
                        recv_sem=rsem.at[way, k - 1],
                        device_id=(lax.rem(me + devices + sign * k, devices),),
                        device_id_type=MESH,
                    )
                )
        return copies

    def unpack(recv):
        half64 = low_half((64, 128))
        half32 = low_half((32, 128))
        half16 = low_half((16, 128))

        def both(value, half):
            other = swap_halves(value)
            return jnp.where(half, value, other), jnp.where(half, other, value)

        for way in range(2):

            def rows(start, size):
                return recv[way, start : start + size, :].astype(F32)

            f1, f2 = both(rows(0, 64), half64)
            f3, f4 = both(rows(64, 64), half64)
            g1, g2 = both(rows(320, 64), half64)
            s1, s2 = both(rows(128, 64), half64)
            d1, d2 = both(rows(192, 32), half32)
            deep = jnp.concatenate([d1, d2], axis=0)
            tiles = {}
            starts = {1: (224, 6), 2: (384, 5), 3: (464, 3), 4: (512, 1)}
            for k, (start, many) in starts.items():
                for j in range(1, many + 1):
                    tiles[k, j] = both(rows(start + 16 * (j - 1), 16), half16)
            n1 = tiles[1, 1][1][8:16]
            c1 = n1
            c2 = c1 + tiles[2, 1][1][8:16]
            c3 = c2 + tiles[3, 1][1][8:16]

            def wide(mask):
                return jnp.concatenate([mask] * 8, axis=0)

            f3 = jnp.where(wide(c1 == 2.0), g1, f3)
            f4 = jnp.where(wide(c1 == 3.0), g1, jnp.where(wide(c1 == 2.0), g2, f4))
            edges, links = [], []
            for t in range(1, WIN + 1):
                e, n = tiles[1, t] if t <= 6 else tiles[4, 1]
                n = n[0:8]
                for j in range(1, 6):
                    if 2 <= t - j <= 6:
                        hit = c1 == float(t - j)
                        e2, n2 = tiles[2, j]
                        e = jnp.where(jnp.concatenate([hit, hit], axis=0), e2, e)
                        n = jnp.where(hit, n2[0:8], n)
                for j in range(1, 4):
                    if t - j >= 4:
                        hit = c2 == float(t - j)
                        e2, n2 = tiles[3, j]
                        e = jnp.where(jnp.concatenate([hit, hit], axis=0), e2, e)
                        n = jnp.where(hit, n2[0:8], n)
                if t == 7:
                    hit = c3 == 6.0
                    e2, n2 = tiles[4, 1]
                    e = jnp.where(jnp.concatenate([hit, hit], axis=0), e2, e)
                    n = jnp.where(hit, n2[0:8], n)
                edges.append(e)
                links.append(n)
            if way == 0:
                for t, f in enumerate((f1, f2, f3, f4), 1):
                    xh[4 - t] = f
                yb[1] = s1
                yb[0] = s2
                zb[0] = deep
                for t in range(1, WIN + 1):
                    eh[WIN - t] = edges[t - 1]
                    lh[WIN - t] = links[t - 1]
            else:
                for t, f in enumerate((f1, f2, f3, f4), 1):
                    xl[SLOTS - 1 + t] = f
                yf[SLOTS] = s1
                yf[SLOTS + 1] = s2
                zf[SLOTS] = deep
                for t in range(1, WIN + 1):
                    el[SLOTS - 1 + t] = edges[t - 1]
                    ll[SLOTS - 1 + t] = links[t - 1]

    def assemble(j):
        held, p, q, r = slot_facts(j)
        q1, r1 = q == 1, r == 1
        dz = jnp.where(r1, -1, 1)
        dy = jnp.where(q1, -2, 2)
        in_low = held & (p > 0)
        in_high = held & (p < last_section)
        zi = lax.broadcasted_iota(jnp.int32, (10, 8, 128), 1)
        bottom, top = zi == 0, zi == 7
        half = low_half((10, 8, 128))

        def put(x, center, side, deep, corner):
            none = jnp.zeros_like(side)
            ten = jnp.concatenate(
                [jnp.where(q1, side, none)[None], center, jnp.where(q1, none, side)[None]], axis=0
            )
            wide = jnp.broadcast_to(corner, (8, 128))
            inner = jnp.broadcast_to(deep[:, None, :], (8, 8, 128))
            row = jnp.concatenate(
                [jnp.where(q1, wide, none)[None], inner, jnp.where(q1, none, wide)[None]], axis=0
            )
            empty = jnp.zeros_like(row)
            before = jnp.where(bottom, jnp.where(r1, row, empty), pltpu.roll(ten, 1, 1))
            after = jnp.where(top, jnp.where(r1, empty, row), pltpu.roll(ten, 7, 1))
            near = jnp.where(half, before, ten)
            both = jnp.concatenate([near, after], axis=2).reshape(80, 256)
            padded[j, x * 80 : (x + 1) * 80, :] = both.astype(BF16)

        def gate(cond, value):
            return jnp.where(cond, value, jnp.zeros_like(value))

        low_at = j + 3
        corner_rows = eh[low_at + dy + dz]
        put(
            0,
            gate(in_low, xh[j]).reshape(8, 8, 128),
            gate(in_low, eh[low_at + dy][0:8]),
            gate(in_low, eh[low_at + dz][8:16]),
            gate(in_low, jnp.where(q1, corner_rows[15:16], corner_rows[8:9])),
        )
        corner_rows = el[forward_index(j + 4 + dy + dz)]
        put(
            9,
            gate(in_high, xl[jnp.minimum(forward_index(j + 4), 9)]).reshape(8, 8, 128),
            gate(in_high, el[forward_index(j + 4 + dy)][0:8]),
            gate(in_high, el[forward_index(j + 4 + dz)][8:16]),
            gate(in_high, jnp.where(q1, corner_rows[15:16], corner_rows[8:9])),
        )
        sides = gate(
            held, jnp.where(q1, yb[j], yf[jnp.minimum(forward_index(j + 2), SLOTS + 1)])
        )
        deeps = gate(held, jnp.where(r1, zb[j], zf[jnp.minimum(forward_index(j + 1), SLOTS)]))
        lines = gate(
            held,
            jnp.where(
                q1,
                lh[7 + j - jnp.where(r1, 3, 1)],
                ll[forward_index(j + jnp.where(r1, 1, 3))],
            ),
        )
        for x in range(8):
            rows = slice(x * 8, x * 8 + 8)
            put(
                x + 1,
                field[j, x * 64 : (x + 1) * 64, :].reshape(8, 8, 128),
                sides[rows],
                deeps[rows],
                lines[x : x + 1],
            )

    last_section = devices * 3 // 4 - 1

    def window(j, a):
        return padded[j, a * 80 : a * 80 + 640, :]

    def combine(total):
        cube = total.reshape(8, 10, 8, 256)
        one = cube[:, 0:8, :, 0:128] + cube[:, 2:10, :, 128:256]
        two = swap_halves(cube[:, 1:9, :, 0:128].reshape(512, 128))
        return one.reshape(512, 128) + two

    @pl.loop(0, SLOTS)
    def _(j):
        value = vox_ref[j].astype(F32)
        field[j] = jnp.concatenate([value, value], axis=0).T
        own_tables(j)

    pack(send1)
    pl.semaphore_wait(barrier, 2 * REACH + plane - 1 + planes - 1)
    first_copies = halo_copies(send1, recv1, ssem1, rsem1)
    for copy in first_copies:
        copy.start()

    acc[...] = jnp.zeros_like(acc)
    bias_acc[...] = jnp.zeros_like(bias_acc)
    bias_row = jnp.concatenate([bias_ref[...], bias_ref[...]], axis=1)

    for copy in first_copies:
        copy.wait_recv()
    unpack(recv1)

    @pl.loop(0, SLOTS)
    def _(j):
        assemble(j)
        total = jnp.dot(window(j, 0), weight_fwd[0], preferred_element_type=F32)
        total += jnp.dot(window(j, 1), weight_fwd[1], preferred_element_type=F32)
        total += jnp.dot(window(j, 2), weight_fwd[2], preferred_element_type=F32)
        pre = (combine(total) + bias_row).T[0:CH]
        held = brick_ref[j] >= 0
        keep = jnp.where(held, cortex_ref[pl.ds(j, 1), :], 0).astype(F32)
        sigma = jax.nn.sigmoid(pre)
        act_ref[j] = (pre * sigma * keep).astype(BF16)
        slope = sigma * (1.0 + pre * (1.0 - sigma))
        grad = (cot_ref[j].astype(F32) * keep * slope).astype(BF16).astype(F32)
        back = jnp.concatenate([grad, grad], axis=0).T
        field[j] = back
        cube = back.reshape(8, 8, 8, 128)
        bias_acc[...] += jnp.sum(back.reshape(64, 8, 128), axis=0)
        gap = jnp.zeros((8, 1, 8, 128), F32)
        zero = jnp.concatenate([cube, gap, gap], axis=1)
        one = jnp.concatenate([gap, cube, gap], axis=1)
        two = jnp.concatenate([gap, gap, cube], axis=1)
        near = jnp.where(low_half((8, 10, 8, 128)), zero, one)
        shifted = jnp.concatenate([near, two], axis=3).reshape(640, 256).astype(BF16)
        turned = shifted.T
        for a in range(3):
            acc[a] += jnp.dot(turned, window(j, a), preferred_element_type=F32)

    lane_group = lax.rem(lanes((GC, 128)), CH) // GC
    half8 = low_half((GC, 128))
    tiles, halves = [], []
    for a in range(3):
        whole = acc[a].T
        for c in range(3):
            one = jnp.zeros((GC, 128), F32)
            two = jnp.zeros((GC, 128), F32)
            for g in range(8):
                rows = slice(c * CH + g * GC, c * CH + (g + 1) * GC)
                one = one + jnp.where(lane_group == g, whole[rows, 0:128], 0.0)
                two = two + jnp.where(lane_group == g, whole[rows, 128:256], 0.0)
            tiles.append(one)
            halves.append(two)
    halves.append(bias_acc[...])
    for i in range(5):
        tiles.append(jnp.where(half8, halves[2 * i], swap_halves(halves[2 * i + 1])))
    chunk = 128 // plane
    for i in range(16):
        tile = tiles[i] if i < 14 else jnp.zeros((GC, 128), F32)
        if chunk == 4:
            part[2 * i] = tile[0:4]
            part[2 * i + 1] = tile[4:8]
        else:
            per = chunk // 8
            part[i // per, (i % per) * 8 : (i % per) * 8 + 8, :] = tile

    def scatter_copy(i):
        to = lax.rem(mine + i, plane)
        return pltpu.make_async_remote_copy(
            src_ref=part.at[to],
            dst_ref=scattered.at[i],
            send_sem=ssem_a.at[i],
            recv_sem=rsem_a.at[i],
            device_id=(plane_peer(i),),
            device_id_type=MESH,
        )

    def level_copy(i, slot):
        return pltpu.make_async_remote_copy(
            src_ref=stacked.at[slot],
            dst_ref=stacked.at[slot],
            send_sem=ssem_b.at[i],
            recv_sem=rsem_b.at[i],
            device_id=(level_peer(i),),
            device_id_type=MESH,
        )

    def gather_copy(i, slot):
        return pltpu.make_async_remote_copy(
            src_ref=final.at[slot],
            dst_ref=final.at[slot],
            send_sem=ssem_c.at[i],
            recv_sem=rsem_c.at[i],
            device_id=(plane_peer(i),),
            device_id_type=MESH,
        )

    @pl.loop(1, plane)
    def _(i):
        scatter_copy(i).start()

    @pl.loop(0, SLOTS)
    def _(j):
        own_tables(j)

    pack(send2)
    second_copies = halo_copies(send2, recv2, ssem2, rsem2)
    for copy in second_copies:
        copy.start()

    @pl.loop(1, plane)
    def _(i):
        scatter_copy(i).wait_recv()

    total = part[mine]
    for i in range(1, plane):
        total = total + scattered[i]
    stacked[level] = total

    @pl.loop(1, planes)
    def _(i):
        level_copy(i, level).start()

    for copy in second_copies:
        copy.wait_recv()
    unpack(recv2)

    def input_gradient(j):
        assemble(j)
        dims = (((1,), (1,)), ((), ()))
        total = lax.dot_general(window(j, 0), weight_bwd[0], dims, preferred_element_type=F32)
        total += lax.dot_general(window(j, 1), weight_bwd[1], dims, preferred_element_type=F32)
        total += lax.dot_general(window(j, 2), weight_bwd[2], dims, preferred_element_type=F32)
        grad_ref[j] = combine(total).T[0:CH].astype(BF16)

    @pl.loop(0, SLOTS // 2)
    def _(j):
        input_gradient(j)

    @pl.loop(1, planes)
    def _(i):
        level_copy(i, lax.rem(level + planes - i, planes)).wait_recv()

    total = stacked[0]
    for i in range(1, planes):
        total = total + stacked[i]
    final[mine] = total

    @pl.loop(1, plane)
    def _(i):
        gather_copy(i, mine).start()

    @pl.loop(SLOTS // 2, SLOTS)
    def _(j):
        input_gradient(j)

    @pl.loop(1, plane)
    def _(i):
        gather_copy(i, lax.rem(mine + plane - i, plane)).wait_recv()

    tiles = []
    for i in range(14):
        if chunk == 4:
            tiles.append(jnp.concatenate([final[2 * i], final[2 * i + 1]], axis=0))
        else:
            per = chunk // 8
            tiles.append(final[i // per, (i % per) * 8 : (i % per) * 8 + 8, :])
    halves = []
    for i in range(5):
        halves.append(tiles[9 + i])
        halves.append(swap_halves(tiles[9 + i]))
    for a in range(3):
        for c in range(3):
            tile = tiles[a * 3 + c]
            kg_ref[a * 9 + c] = tile[:, 0:CH]
            kg_ref[a * 9 + 3 + c] = swap_halves(tile)[:, 0:CH]
            kg_ref[a * 9 + 6 + c] = halves[a * 3 + c][:, 0:CH]
    bg_ref[...] = jnp.sum(halves[9], axis=0, keepdims=True)[:, 0:CH]

    for copy in first_copies:
        copy.wait_send()
    for copy in second_copies:
        copy.wait_send()

    @pl.loop(1, plane)
    def _(i):
        scatter_copy(i).wait_send()
        gather_copy(i, mine).wait_send()

    @pl.loop(1, planes)
    def _(i):
        level_copy(i, level).wait_send()


def shards(devices, voxels, kernel, bias, cortex, slot_to_brick, neighbors, cotangent):
    plane = plane_size(devices)
    planes = devices // plane
    chunk = 128 // plane
    taps = jnp.transpose(kernel, (2, 3, 4, 1, 0)).reshape(27, GC, CH)
    vmem = pl.BlockSpec(memory_space=pltpu.VMEM)
    dma = pltpu.SemaphoreType.DMA
    act, grad, kg, bg = pl.pallas_call(
        functools.partial(kernel_body, devices, planes),
        out_shape=(
            jax.ShapeDtypeStruct((SLOTS, CH, V), BF16),
            jax.ShapeDtypeStruct((SLOTS, CH, V), BF16),
            jax.ShapeDtypeStruct((27, GC, CH), F32),
            jax.ShapeDtypeStruct((1, CH), F32),
        ),
        in_specs=[pl.BlockSpec(memory_space=pltpu.SMEM)] + [vmem] * 5,
        out_specs=(vmem,) * 4,
        scratch_shapes=[
            pltpu.VMEM((SLOTS, V, 128), F32),
            pltpu.VMEM((SLOTS, 800, 256), BF16),
            pltpu.VMEM((3, 256, 256), BF16),
            pltpu.VMEM((3, 256, 256), BF16),
            pltpu.VMEM((10, 64, 128), F32),
            pltpu.VMEM((10, 64, 128), F32),
            pltpu.VMEM((8, 64, 128), F32),
            pltpu.VMEM((8, 64, 128), F32),
            pltpu.VMEM((7, 64, 128), F32),
            pltpu.VMEM((7, 64, 128), F32),
            pltpu.VMEM((13, 16, 128), F32),
            pltpu.VMEM((13, 16, 128), F32),
            pltpu.VMEM((13, 8, 128), F32),
            pltpu.VMEM((13, 8, 128), F32),
            pltpu.VMEM((2, MSG_TOTAL, 128), BF16),
            pltpu.VMEM((2, MSG_TOTAL, 128), BF16),
            pltpu.VMEM((2, MSG_TOTAL, 128), BF16),
            pltpu.VMEM((2, MSG_TOTAL, 128), BF16),
            pltpu.VMEM((3, 256, 256), F32),
            pltpu.VMEM((GC, 128), F32),
            pltpu.VMEM((plane, chunk, 128), F32),
            pltpu.VMEM((plane, chunk, 128), F32),
            pltpu.VMEM((planes, chunk, 128), F32),
            pltpu.VMEM((plane, chunk, 128), F32),
            dma((2, REACH)),
            dma((2, REACH)),
            dma((2, REACH)),
            dma((2, REACH)),
            dma((plane,)),
            dma((plane,)),
            dma((planes,)),
            dma((planes,)),
            dma((plane,)),
            dma((plane,)),
        ],
        compiler_params=pltpu.CompilerParams(
            collective_id=0, has_side_effects=True, vmem_limit_bytes=60 * 1024 * 1024
        ),
    )(slot_to_brick, voxels, cotangent, cortex, taps, bias.reshape(1, CH))
    kernel_grad = jnp.transpose(kg.reshape(3, 3, 3, GC, CH), (4, 3, 0, 1, 2))
    return (act, grad, kernel_grad, bg.reshape(CH))


def solution(mesh):
    devices = mesh.shape[AXIS]
    return jax.shard_map(
        functools.partial(shards, devices),
        mesh=mesh,
        in_specs=(
            P(AXIS, None, None),
            P(),
            P(),
            P(AXIS, None),
            P(AXIS),
            P(AXIS, None),
            P(AXIS, None, None),
        ),
        out_specs=(P(AXIS, None, None), P(AXIS, None, None), P(), P()),
        check_vma=False,
    )
```

```python
import functools

import jax
import jax.numpy as jnp
from jax import lax
from jax.experimental import pallas as pl
from jax.experimental.pallas import tpu as pltpu
from jax.sharding import PartitionSpec as P

AXIS = "bricks"
CH = 64
GC = 8
V = 512
SLOTS = 6
REACH = 4
WIN = 7
MSG_ROWS = (320, 144, 48, 16)
MSG_BASE = (0, 320, 464, 512)
MSG_TOTAL = 528
F32 = jnp.float32
BF16 = jnp.bfloat16
MESH = pl.DeviceIdType.MESH


def plane_size(devices):
    return 32 if devices >= 64 else devices // 2


def lanes(shape):
    return lax.broadcasted_iota(jnp.int32, shape, len(shape) - 1)


def low_half(shape):
    return lanes(shape) < CH


def swap_halves(value):
    return pltpu.roll(value, CH, value.ndim - 1)


def kernel_body(
    devices,
    planes,
    brick_ref,
    vox_ref,
    cot_ref,
    cortex_ref,
    taps_ref,
    bias_ref,
    act_ref,
    grad_ref,
    kg_ref,
    bg_ref,
    field,
    padded,
    spread_grad,
    weight_fwd,
    weight_bwd,
    xh,
    xl,
    yb,
    yf,
    zb,
    zf,
    eh,
    el,
    lh,
    ll,
    send1,
    recv1,
    send2,
    recv2,
    part,
    scattered,
    stacked,
    final,
    ssem1,
    rsem1,
    ssem2,
    rsem2,
    ssem_a,
    rsem_a,
    ssem_b,
    rsem_b,
    ssem_c,
    rsem_c,
):
    plane = plane_size(devices)
    me = lax.axis_index(AXIS)
    mine = lax.rem(me, plane)
    level = me // plane

    def plane_peer(i):
        return level * plane + lax.rem(mine + i, plane)

    def level_peer(i):
        return lax.rem(level + i, planes) * plane + mine

    barrier = pltpu.get_barrier_semaphore()
    def reached(sign, k):
        return me + k < devices if sign > 0 else me >= k

    for k in range(1, REACH + 1):
        for sign in (-1, 1):

            @pl.when(reached(sign, k))
            def _():
                pl.semaphore_signal(
                    barrier, inc=1, device_id=(me + sign * k,), device_id_type=MESH
                )

    @pl.loop(1, plane)
    def _(i):
        pl.semaphore_signal(barrier, inc=1, device_id=(plane_peer(i),), device_id_type=MESH)

    @pl.loop(1, planes)
    def _(i):
        pl.semaphore_signal(barrier, inc=1, device_id=(level_peer(i),), device_id_type=MESH)

    first = brick_ref[0]
    count = jnp.int32(0)
    for j in range(SLOTS):
        count = count + jnp.where(brick_ref[j] >= 0, 1, 0).astype(jnp.int32)

    def forward_index(m):
        return jnp.minimum(jnp.where(m < count, m, SLOTS + m - count), 12)

    row_group = lax.broadcasted_iota(jnp.int32, (CH, 128), 0) // GC
    col_group = lax.rem(lanes((CH, 128)), CH) // GC
    same_group = row_group == col_group
    left = low_half((CH, 128))
    zero_half = jnp.zeros((GC, CH), F32)

    def spread(first_tap, second_tap):
        one = taps_ref[first_tap].astype(F32)
        two = zero_half if second_tap is None else taps_ref[second_tap].astype(F32)
        both = jnp.concatenate([one, two], axis=1)
        return jnp.where(same_group, jnp.concatenate([both] * GC, axis=0), 0.0).astype(BF16)

    blank = jnp.zeros((CH, 256), BF16)
    for a in range(3):
        for c in range(3):
            rows = slice(c * CH, (c + 1) * CH)
            weight_fwd[a, rows, 0:128] = spread(a * 9 + c, a * 9 + 3 + c)
            weight_fwd[a, rows, 128:256] = spread(a * 9 + 6 + c, None)
        weight_fwd[a, 3 * CH : 4 * CH, :] = blank
        for b in range(3):
            rows = slice(b * CH, (b + 1) * CH)
            base = (2 - a) * 9 + (2 - b) * 3
            weight_bwd[a, rows, 0:128] = spread(base + 2, base + 1)
            weight_bwd[a, rows, 128:256] = spread(base, None)
        weight_bwd[a, 3 * CH : 4 * CH, :] = blank

    def slot_facts(j):
        brick = brick_ref[j]
        held = brick >= 0
        safe = jnp.maximum(brick, 0)
        return held, safe // 4, lax.rem(safe // 2, 2), lax.rem(safe, 2)

    def own_tables(j):
        held, _, q, r = slot_facts(j)
        q0, r0 = q == 0, r == 0
        high = field[j, 448:512, :]
        low = field[j, 0:64, :]
        xh[j + 4] = high
        xl[j] = low
        cube = field[j].reshape(8, 8, 8, 128)
        side = jnp.where(q0, cube[:, 7], cube[:, 0]).reshape(64, 128)
        yb[j + 2] = side
        yf[j] = side
        deep = jnp.where(
            r0, field[j, pl.ds(7, 64, stride=8), :], field[j, pl.ds(0, 64, stride=8), :]
        )
        zb[j + 1] = deep
        zf[j] = deep
        for table, at, start in ((eh, j + 7, 448), (el, j, 0)):
            table[at, 0:8, :] = jnp.where(
                q0, field[j, start + 56 : start + 64, :], field[j, start : start + 8, :]
            )
            table[at, 8:16, :] = jnp.where(
                r0,
                field[j, pl.ds(start + 7, 8, stride=8), :],
                field[j, pl.ds(start, 8, stride=8), :],
            )
        line = jnp.where(
            q0,
            jnp.where(
                r0,
                field[j, pl.ds(63, 8, stride=64), :],
                field[j, pl.ds(56, 8, stride=64), :],
            ),
            jnp.where(
                r0,
                field[j, pl.ds(7, 8, stride=64), :],
                field[j, pl.ds(0, 8, stride=64), :],
            ),
        )
        lh[j + 7] = line
        ll[j] = line

    def pack(send):
        half64 = low_half((64, 128))
        half32 = low_half((32, 128))
        half8 = low_half((8, 128))
        number = jnp.zeros((8, 128), F32) + count.astype(F32)
        for way in range(2):
            if way == 0:
                face, side, deep, edge, line = xh, yb, zb, eh, lh

                def at(table, j, ahead):
                    return table[ahead + jnp.maximum(count - j, 0)]

                shifts = (4, 2, 1, 7, 7)
            else:
                face, side, deep, edge, line = xl, yf, zf, el, ll

                def at(table, j, ahead):
                    return table[j - 1]

                shifts = (0, 0, 0, 0, 0)

            def pair(one, two):
                return jnp.where(half64, one, two).astype(BF16)

            f = [at(face, j, shifts[0]) for j in range(1, 5)]
            send[way, 0:64, :] = pair(f[0], f[1])
            send[way, 64:128, :] = pair(f[2], f[3])
            send[way, 128:192, :] = pair(at(side, 1, shifts[1]), at(side, 2, shifts[1]))
            d = at(deep, 1, shifts[2])
            send[way, 192:224, :] = jnp.where(half32, d[0:32], d[32:64]).astype(BF16)
            send[way, 320:384, :] = pair(f[0], f[1])
            for j in range(1, 7):
                e = at(edge, j, shifts[3])
                n = at(line, j, shifts[4])
                tile = jnp.concatenate(
                    [jnp.where(half8, e[0:8], n), jnp.where(half8, e[8:16], number)], axis=0
                ).astype(BF16)
                send[way, 224 + 16 * (j - 1) : 240 + 16 * (j - 1), :] = tile
                if j <= 5:
                    send[way, 384 + 16 * (j - 1) : 400 + 16 * (j - 1), :] = tile
                if j <= 3:
                    send[way, 464 + 16 * (j - 1) : 480 + 16 * (j - 1), :] = tile
                if j == 1:
                    send[way, 512:528, :] = tile

    def halo_copies(send, recv, ssem, rsem):
        copies = []
        for way, sign in ((0, 1), (1, -1)):
            for k in range(1, REACH + 1):
                rows = pl.ds(MSG_BASE[k - 1], MSG_ROWS[k - 1])
                copies.append(
                    pltpu.make_async_remote_copy(
                        src_ref=send.at[way, rows, :],
                        dst_ref=recv.at[way, rows, :],
                        send_sem=ssem.at[way, k - 1],
                        recv_sem=rsem.at[way, k - 1],
                        device_id=(jnp.clip(me + sign * k, 0, devices - 1),),
                        device_id_type=MESH,
                    )
                )
        return copies

    def each_sent(copies, act):
        for i, copy in enumerate(copies):
            sign = 1 if i < REACH else -1

            @pl.when(reached(sign, i % REACH + 1))
            def _():
                act(copy)

    def each_received(copies):
        for i, copy in enumerate(copies):
            sign = 1 if i < REACH else -1

            @pl.when(reached(-sign, i % REACH + 1))
            def _():
                copy.wait_recv()

    def unpack(recv):
        half64 = low_half((64, 128))
        half32 = low_half((32, 128))
        half16 = low_half((16, 128))

        def both(value, half):
            other = swap_halves(value)
            return jnp.where(half, value, other), jnp.where(half, other, value)

        for way in range(2):

            def rows(start, size):
                return recv[way, start : start + size, :].astype(F32)

            f1, f2 = both(rows(0, 64), half64)
            f3, f4 = both(rows(64, 64), half64)
            g1, g2 = both(rows(320, 64), half64)
            s1, s2 = both(rows(128, 64), half64)
            d1, d2 = both(rows(192, 32), half32)
            deep = jnp.concatenate([d1, d2], axis=0)
            tiles = {}
            starts = {1: (224, 6), 2: (384, 5), 3: (464, 3), 4: (512, 1)}
            for k, (start, many) in starts.items():
                for j in range(1, many + 1):
                    tiles[k, j] = both(rows(start + 16 * (j - 1), 16), half16)
            n1 = tiles[1, 1][1][8:16]
            c1 = n1
            c2 = c1 + tiles[2, 1][1][8:16]
            c3 = c2 + tiles[3, 1][1][8:16]

            def wide(mask):
                return jnp.concatenate([mask] * 8, axis=0)

            f3 = jnp.where(wide(c1 == 2.0), g1, f3)
            f4 = jnp.where(wide(c1 == 3.0), g1, jnp.where(wide(c1 == 2.0), g2, f4))
            edges, links = [], []
            for t in range(1, WIN + 1):
                e, n = tiles[1, t] if t <= 6 else tiles[4, 1]
                n = n[0:8]
                for j in range(1, 6):
                    if 2 <= t - j <= 6:
                        hit = c1 == float(t - j)
                        e2, n2 = tiles[2, j]
                        e = jnp.where(jnp.concatenate([hit, hit], axis=0), e2, e)
                        n = jnp.where(hit, n2[0:8], n)
                for j in range(1, 4):
                    if t - j >= 4:
                        hit = c2 == float(t - j)
                        e2, n2 = tiles[3, j]
                        e = jnp.where(jnp.concatenate([hit, hit], axis=0), e2, e)
                        n = jnp.where(hit, n2[0:8], n)
                if t == 7:
                    hit = c3 == 6.0
                    e2, n2 = tiles[4, 1]
                    e = jnp.where(jnp.concatenate([hit, hit], axis=0), e2, e)
                    n = jnp.where(hit, n2[0:8], n)
                edges.append(e)
                links.append(n)
            if way == 0:
                for t, f in enumerate((f1, f2, f3, f4), 1):
                    xh[4 - t] = f
                yb[1] = s1
                yb[0] = s2
                zb[0] = deep
                for t in range(1, WIN + 1):
                    eh[WIN - t] = edges[t - 1]
                    lh[WIN - t] = links[t - 1]
            else:
                for t, f in enumerate((f1, f2, f3, f4), 1):
                    xl[SLOTS - 1 + t] = f
                yf[SLOTS] = s1
                yf[SLOTS + 1] = s2
                zf[SLOTS] = deep
                for t in range(1, WIN + 1):
                    el[SLOTS - 1 + t] = edges[t - 1]
                    ll[SLOTS - 1 + t] = links[t - 1]

    def assemble(j):
        held, p, q, r = slot_facts(j)
        q1, r1 = q == 1, r == 1
        dz = jnp.where(r1, -1, 1)
        dy = jnp.where(q1, -2, 2)
        in_low = held & (p > 0)
        in_high = held & (p < last_section)
        zi = lax.broadcasted_iota(jnp.int32, (10, 8, 128), 1)
        bottom, top = zi == 0, zi == 7
        half = low_half((10, 8, 128))

        def put(x, center, side, deep, corner):
            none = jnp.zeros_like(side)
            ten = jnp.concatenate(
                [jnp.where(q1, side, none)[None], center, jnp.where(q1, none, side)[None]], axis=0
            )
            wide = jnp.broadcast_to(corner, (8, 128))
            inner = jnp.broadcast_to(deep[:, None, :], (8, 8, 128))
            row = jnp.concatenate(
                [jnp.where(q1, wide, none)[None], inner, jnp.where(q1, none, wide)[None]], axis=0
            )
            empty = jnp.zeros_like(row)
            before = jnp.where(bottom, jnp.where(r1, row, empty), pltpu.roll(ten, 1, 1))
            after = jnp.where(top, jnp.where(r1, empty, row), pltpu.roll(ten, 7, 1))
            near = jnp.where(half, before, ten)
            both = jnp.concatenate([near, after], axis=2).reshape(80, 256)
            padded[x, j] = both.astype(BF16)

        def gate(cond, value):
            return jnp.where(cond, value, jnp.zeros_like(value))

        low_at = j + 3
        corner_rows = eh[low_at + dy + dz]
        put(
            0,
            gate(in_low, xh[j]).reshape(8, 8, 128),
            gate(in_low, eh[low_at + dy][0:8]),
            gate(in_low, eh[low_at + dz][8:16]),
            gate(in_low, jnp.where(q1, corner_rows[15:16], corner_rows[8:9])),
        )
        corner_rows = el[forward_index(j + 4 + dy + dz)]
        put(
            9,
            gate(in_high, xl[jnp.minimum(forward_index(j + 4), 9)]).reshape(8, 8, 128),
            gate(in_high, el[forward_index(j + 4 + dy)][0:8]),
            gate(in_high, el[forward_index(j + 4 + dz)][8:16]),
            gate(in_high, jnp.where(q1, corner_rows[15:16], corner_rows[8:9])),
        )
        sides = gate(
            held, jnp.where(q1, yb[j], yf[jnp.minimum(forward_index(j + 2), SLOTS + 1)])
        )
        deeps = gate(held, jnp.where(r1, zb[j], zf[jnp.minimum(forward_index(j + 1), SLOTS)]))
        lines = gate(
            held,
            jnp.where(
                q1,
                lh[7 + j - jnp.where(r1, 3, 1)],
                ll[forward_index(j + jnp.where(r1, 1, 3))],
            ),
        )
        for x in range(8):
            rows = slice(x * 8, x * 8 + 8)
            put(
                x + 1,
                field[j, x * 64 : (x + 1) * 64, :].reshape(8, 8, 128),
                sides[rows],
                deeps[rows],
                lines[x : x + 1],
            )

    last_section = devices * 3 // 4 - 1

    def window(j, a):
        return padded[a : a + 8, j].reshape(640, 256)

    def combine(total):
        cube = total.reshape(8, 10, 8, 256)
        one = cube[:, 0:8, :, 0:128] + cube[:, 2:10, :, 128:256]
        two = swap_halves(cube[:, 1:9, :, 0:128].reshape(512, 128))
        return one.reshape(512, 128) + two

    @pl.loop(0, SLOTS)
    def _(j):
        value = vox_ref[j].astype(F32)
        field[j] = jnp.concatenate([value, value], axis=0).T
        own_tables(j)

    pack(send1)
    chain = jnp.minimum(me, REACH) + jnp.minimum(devices - 1 - me, REACH)
    pl.semaphore_wait(barrier, chain + plane - 1 + planes - 1)
    first_copies = halo_copies(send1, recv1, ssem1, rsem1)
    each_sent(first_copies, lambda copy: copy.start())

    bias_row = jnp.concatenate([bias_ref[...], bias_ref[...]], axis=1)

    each_received(first_copies)
    unpack(recv1)

    def forward(j):
        total = jnp.dot(window(j, 0), weight_fwd[0], preferred_element_type=F32)
        total += jnp.dot(window(j, 1), weight_fwd[1], preferred_element_type=F32)
        total += jnp.dot(window(j, 2), weight_fwd[2], preferred_element_type=F32)
        return (combine(total) + bias_row).T[0:CH]

    def slopes(j, pre):
        held = brick_ref[j] >= 0
        keep = jnp.where(held, cortex_ref[j : j + 1, :], 0).astype(F32)
        sigma = jax.nn.sigmoid(pre)
        act_ref[j] = (pre * sigma * keep).astype(BF16)
        slope = sigma * (1.0 + pre * (1.0 - sigma))
        grad = (cot_ref[j].astype(F32) * keep * slope).astype(BF16).astype(F32)
        back = jnp.concatenate([grad, grad], axis=0).T
        field[j] = back
        cube = back.reshape(8, 8, 8, 128)
        gap = jnp.zeros((8, 1, 8, 128), F32)
        zero = jnp.concatenate([cube, gap, gap], axis=1)
        one = jnp.concatenate([gap, cube, gap], axis=1)
        two = jnp.concatenate([gap, gap, cube], axis=1)
        near = jnp.where(low_half((8, 10, 8, 128)), zero, one)
        shifted = jnp.concatenate([near, two], axis=3).reshape(8, 80, 256).astype(BF16)
        for x in range(8):
            spread_grad[x, j] = shifted[x]
        return jnp.sum(back.reshape(64, 8, 128), axis=0)

    bias_part = jnp.zeros((GC, 128), F32)
    for j in range(SLOTS):
        assemble(j)
    for j in range(SLOTS):
        bias_part = bias_part + slopes(j, forward(j))
    turned = spread_grad[...].reshape(8 * SLOTS * 80, 256).T
    whole_grad = [
        jnp.dot(
            turned,
            padded[a : a + 8].reshape(8 * SLOTS * 80, 256),
            preferred_element_type=F32,
        )
        for a in range(3)
    ]

    lane_group = lax.rem(lanes((GC, 128)), CH) // GC
    half8 = low_half((GC, 128))
    tiles, halves = [], []
    for a in range(3):
        whole = whole_grad[a].T
        for c in range(3):
            one = jnp.zeros((GC, 128), F32)
            two = jnp.zeros((GC, 128), F32)
            for g in range(8):
                rows = slice(c * CH + g * GC, c * CH + (g + 1) * GC)
                one = one + jnp.where(lane_group == g, whole[rows, 0:128], 0.0)
                two = two + jnp.where(lane_group == g, whole[rows, 128:256], 0.0)
            tiles.append(one)
            halves.append(two)
    halves.append(bias_part)
    for i in range(5):
        tiles.append(jnp.where(half8, halves[2 * i], swap_halves(halves[2 * i + 1])))
    chunk = 128 // plane
    for i in range(16):
        tile = tiles[i] if i < 14 else jnp.zeros((GC, 128), F32)
        if chunk == 4:
            part[2 * i] = tile[0:4]
            part[2 * i + 1] = tile[4:8]
        else:
            per = chunk // 8
            part[i // per, (i % per) * 8 : (i % per) * 8 + 8, :] = tile

    def scatter_copy(i):
        to = lax.rem(mine + i, plane)
        return pltpu.make_async_remote_copy(
            src_ref=part.at[to],
            dst_ref=scattered.at[i],
            send_sem=ssem_a.at[i],
            recv_sem=rsem_a.at[i],
            device_id=(plane_peer(i),),
            device_id_type=MESH,
        )

    def level_copy(i, slot):
        return pltpu.make_async_remote_copy(
            src_ref=stacked.at[slot],
            dst_ref=stacked.at[slot],
            send_sem=ssem_b.at[i],
            recv_sem=rsem_b.at[i],
            device_id=(level_peer(i),),
            device_id_type=MESH,
        )

    def gather_copy(i, slot):
        return pltpu.make_async_remote_copy(
            src_ref=final.at[slot],
            dst_ref=final.at[slot],
            send_sem=ssem_c.at[i],
            recv_sem=rsem_c.at[i],
            device_id=(plane_peer(i),),
            device_id_type=MESH,
        )

    @pl.loop(1, plane)
    def _(i):
        scatter_copy(i).start()

    @pl.loop(1, plane)
    def _(i):
        scatter_copy(i).wait_recv()

    total = part[mine]
    for i in range(1, plane):
        total = total + scattered[i]
    stacked[level] = total

    @pl.loop(1, planes)
    def _(i):
        level_copy(i, level).start()

    @pl.loop(0, SLOTS)
    def _(j):
        own_tables(j)

    pack(send2)
    second_copies = halo_copies(send2, recv2, ssem2, rsem2)
    each_sent(second_copies, lambda copy: copy.start())

    each_received(second_copies)
    unpack(recv2)

    def input_gradient(j):
        assemble(j)
        dims = (((1,), (1,)), ((), ()))
        total = lax.dot_general(window(j, 0), weight_bwd[0], dims, preferred_element_type=F32)
        total += lax.dot_general(window(j, 1), weight_bwd[1], dims, preferred_element_type=F32)
        total += lax.dot_general(window(j, 2), weight_bwd[2], dims, preferred_element_type=F32)
        grad_ref[j] = combine(total).T[0:CH].astype(BF16)

    @pl.loop(0, SLOTS // 2)
    def _(j):
        input_gradient(j)

    @pl.loop(1, planes)
    def _(i):
        level_copy(i, lax.rem(level + planes - i, planes)).wait_recv()

    total = stacked[0]
    for i in range(1, planes):
        total = total + stacked[i]
    final[mine] = total

    @pl.loop(1, plane)
    def _(i):
        gather_copy(i, mine).start()

    @pl.loop(SLOTS // 2, SLOTS)
    def _(j):
        input_gradient(j)

    @pl.loop(1, plane)
    def _(i):
        gather_copy(i, lax.rem(mine + plane - i, plane)).wait_recv()

    tiles = []
    for i in range(14):
        if chunk == 4:
            tiles.append(jnp.concatenate([final[2 * i], final[2 * i + 1]], axis=0))
        else:
            per = chunk // 8
            tiles.append(final[i // per, (i % per) * 8 : (i % per) * 8 + 8, :])
    halves = []
    for i in range(5):
        halves.append(tiles[9 + i])
        halves.append(swap_halves(tiles[9 + i]))
    for a in range(3):
        for c in range(3):
            tile = tiles[a * 3 + c]
            kg_ref[a * 9 + c] = tile[:, 0:CH]
            kg_ref[a * 9 + 3 + c] = swap_halves(tile)[:, 0:CH]
            kg_ref[a * 9 + 6 + c] = halves[a * 3 + c][:, 0:CH]
    bg_ref[...] = jnp.sum(halves[9], axis=0, keepdims=True)[:, 0:CH]

    each_sent(first_copies, lambda copy: copy.wait_send())
    each_sent(second_copies, lambda copy: copy.wait_send())

    @pl.loop(1, plane)
    def _(i):
        scatter_copy(i).wait_send()
        gather_copy(i, mine).wait_send()

    @pl.loop(1, planes)
    def _(i):
        level_copy(i, level).wait_send()


def copy_body(*refs):
    sources, targets, sem = refs[:4], refs[4:8], refs[8]
    copies = [
        pltpu.make_async_copy(source, target, sem.at[i])
        for i, (source, target) in enumerate(zip(sources, targets))
    ]
    for copy in copies:
        copy.start()
    for copy in copies:
        copy.wait()


def write_out(*values):
    return pl.pallas_call(
        copy_body,
        out_shape=tuple(jax.ShapeDtypeStruct(v.shape, v.dtype) for v in values),
        in_specs=[pl.BlockSpec(memory_space=pltpu.VMEM)] * 4,
        out_specs=(pl.BlockSpec(memory_space=pl.ANY),) * 4,
        scratch_shapes=[pltpu.SemaphoreType.DMA((4,))],
    )(*[pltpu.with_memory_space_constraint(v, pltpu.VMEM) for v in values])


def shards(devices, voxels, kernel, bias, cortex, slot_to_brick, neighbors, cotangent):
    plane = plane_size(devices)
    planes = devices // plane
    chunk = 128 // plane
    taps = jnp.transpose(kernel, (2, 3, 4, 1, 0)).reshape(27, GC, CH)
    vmem = pl.BlockSpec(memory_space=pltpu.VMEM)
    dma = pltpu.SemaphoreType.DMA
    act, grad, kg, bg = pl.pallas_call(
        functools.partial(kernel_body, devices, planes),
        out_shape=(
            pltpu.VMEM((SLOTS, CH, V), BF16),
            pltpu.VMEM((SLOTS, CH, V), BF16),
            pltpu.VMEM((27, GC, CH), F32),
            pltpu.VMEM((1, CH), F32),
        ),
        in_specs=[pl.BlockSpec(memory_space=pltpu.SMEM)] + [vmem] * 5,
        out_specs=(vmem,) * 4,
        scratch_shapes=[
            pltpu.VMEM((SLOTS, V, 128), F32),
            pltpu.VMEM((10, SLOTS, 80, 256), BF16),
            pltpu.VMEM((8, SLOTS, 80, 256), BF16),
            pltpu.VMEM((3, 256, 256), BF16),
            pltpu.VMEM((3, 256, 256), BF16),
            pltpu.VMEM((10, 64, 128), F32),
            pltpu.VMEM((10, 64, 128), F32),
            pltpu.VMEM((8, 64, 128), F32),
            pltpu.VMEM((8, 64, 128), F32),
            pltpu.VMEM((7, 64, 128), F32),
            pltpu.VMEM((7, 64, 128), F32),
            pltpu.VMEM((13, 16, 128), F32),
            pltpu.VMEM((13, 16, 128), F32),
            pltpu.VMEM((13, 8, 128), F32),
            pltpu.VMEM((13, 8, 128), F32),
            pltpu.VMEM((2, MSG_TOTAL, 128), BF16),
            pltpu.VMEM((2, MSG_TOTAL, 128), BF16),
            pltpu.VMEM((2, MSG_TOTAL, 128), BF16),
            pltpu.VMEM((2, MSG_TOTAL, 128), BF16),
            pltpu.VMEM((plane, chunk, 128), F32),
            pltpu.VMEM((plane, chunk, 128), F32),
            pltpu.VMEM((planes, chunk, 128), F32),
            pltpu.VMEM((plane, chunk, 128), F32),
            dma((2, REACH)),
            dma((2, REACH)),
            dma((2, REACH)),
            dma((2, REACH)),
            dma((plane,)),
            dma((plane,)),
            dma((planes,)),
            dma((planes,)),
            dma((plane,)),
            dma((plane,)),
        ],
        compiler_params=pltpu.CompilerParams(
            collective_id=0, has_side_effects=True, vmem_limit_bytes=60 * 1024 * 1024
        ),
    )(slot_to_brick, voxels, cotangent, cortex, taps, bias.reshape(1, CH))
    act, grad, kg, bg = write_out(act, grad, kg, bg)
    kernel_grad = jnp.transpose(kg.reshape(3, 3, 3, GC, CH), (4, 3, 0, 1, 2))
    return (act, grad, kernel_grad, bg.reshape(CH))


def solution(mesh):
    devices = mesh.shape[AXIS]
    return jax.shard_map(
        functools.partial(shards, devices),
        mesh=mesh,
        in_specs=(
            P(AXIS, None, None),
            P(),
            P(),
            P(AXIS, None),
            P(AXIS),
            P(AXIS, None),
            P(AXIS, None, None),
        ),
        out_specs=(P(AXIS, None, None), P(AXIS, None, None), P(), P()),
        check_vma=False,
    )
```

```python
import functools

import jax
import jax.numpy as jnp
from jax import lax
from jax.experimental import pallas as pl
from jax.experimental.pallas import tpu as pltpu
from jax.sharding import PartitionSpec as P

AXIS = "bricks"
CH = 64
GC = 8
V = 512
SLOTS = 6
REACH = 4
WIN = 7
MSG_ROWS = (320, 144, 48, 16)
MSG_BASE = (0, 320, 464, 512)
MSG_TOTAL = 528
F32 = jnp.float32
BF16 = jnp.bfloat16
MESH = pl.DeviceIdType.MESH


def plane_size(devices):
    return 32 if devices >= 64 else devices // 2


def lanes(shape):
    return lax.broadcasted_iota(jnp.int32, shape, len(shape) - 1)


def low_half(shape):
    return lanes(shape) < CH


def swap_halves(value):
    return pltpu.roll(value, CH, value.ndim - 1)


def kernel_body(
    devices,
    planes,
    brick_ref,
    vox_hbm,
    cot_hbm,
    cortex_hbm,
    taps_hbm,
    bias_hbm,
    act_ref,
    grad_ref,
    kg_ref,
    bg_ref,
    vox_ref,
    cot_ref,
    cortex_ref,
    taps_ref,
    bias_ref,
    field,
    padded,
    spread_grad,
    pre_ref,
    acc,
    bias_acc,
    weight_fwd,
    weight_bwd,
    xh,
    xl,
    yb,
    yf,
    zb,
    zf,
    eh,
    el,
    lh,
    ll,
    send1,
    recv1,
    send2,
    recv2,
    part,
    scattered,
    stacked,
    final,
    ssem1,
    rsem1,
    ssem2,
    rsem2,
    sems,
    loads,
):
    plane = plane_size(devices)
    me = lax.axis_index(AXIS)
    mine = lax.rem(me, plane)
    level = me // plane

    def plane_peer(i):
        return level * plane + lax.rem(mine + i, plane)

    def level_peer(i):
        return lax.rem(level + i, planes) * plane + mine

    barrier = pltpu.get_barrier_semaphore()
    def reached(sign, k):
        return me + k < devices if sign > 0 else me >= k

    for k in range(1, REACH + 1):
        for sign in (-1, 1):

            @pl.when(reached(sign, k))
            def _():
                pl.semaphore_signal(
                    barrier, inc=1, device_id=(me + sign * k,), device_id_type=MESH
                )

    @pl.loop(1, plane)
    def _(i):
        pl.semaphore_signal(barrier, inc=1, device_id=(plane_peer(i),), device_id_type=MESH)

    @pl.loop(1, planes)
    def _(i):
        pl.semaphore_signal(barrier, inc=1, device_id=(level_peer(i),), device_id_type=MESH)

    fetches = [
        pltpu.make_async_copy(source, target, loads.at[i])
        for i, (source, target) in enumerate(
            (
                (vox_hbm, vox_ref),
                (taps_hbm, taps_ref),
                (cot_hbm, cot_ref),
                (cortex_hbm, cortex_ref),
                (bias_hbm, bias_ref),
            )
        )
    ]
    for fetch in fetches:
        fetch.start()

    count = jnp.int32(0)
    for j in range(SLOTS):
        count = count + jnp.where(brick_ref[j] >= 0, 1, 0).astype(jnp.int32)

    def forward_index(m):
        return jnp.minimum(jnp.where(m < count, m, SLOTS + m - count), 12)

    def slot_facts(j):
        brick = brick_ref[j]
        held = brick >= 0
        safe = jnp.maximum(brick, 0)
        return held, safe // 4, lax.rem(safe // 2, 2), lax.rem(safe, 2)

    def own_tables(j):
        held, _, q, r = slot_facts(j)
        q0, r0 = q == 0, r == 0
        high = field[j, 448:512, :]
        low = field[j, 0:64, :]
        xh[j + 4] = high
        xl[j] = low
        cube = field[j].reshape(8, 8, 8, 128)
        side = jnp.where(q0, cube[:, 7], cube[:, 0]).reshape(64, 128)
        yb[j + 2] = side
        yf[j] = side
        deep = jnp.where(
            r0, field[j, pl.ds(7, 64, stride=8), :], field[j, pl.ds(0, 64, stride=8), :]
        )
        zb[j + 1] = deep
        zf[j] = deep
        for table, at, start in ((eh, j + 7, 448), (el, j, 0)):
            table[at, 0:8, :] = jnp.where(
                q0, field[j, start + 56 : start + 64, :], field[j, start : start + 8, :]
            )
            table[at, 8:16, :] = jnp.where(
                r0,
                field[j, pl.ds(start + 7, 8, stride=8), :],
                field[j, pl.ds(start, 8, stride=8), :],
            )
        line = jnp.where(
            q0,
            jnp.where(
                r0,
                field[j, pl.ds(63, 8, stride=64), :],
                field[j, pl.ds(56, 8, stride=64), :],
            ),
            jnp.where(
                r0,
                field[j, pl.ds(7, 8, stride=64), :],
                field[j, pl.ds(0, 8, stride=64), :],
            ),
        )
        lh[j + 7] = line
        ll[j] = line

    def pack(send):
        half64 = low_half((64, 128))
        half32 = low_half((32, 128))
        half8 = low_half((8, 128))
        number = jnp.zeros((8, 128), F32) + count.astype(F32)
        for way in range(2):
            if way == 0:
                face, side, deep, edge, line = xh, yb, zb, eh, lh

                def at(table, j, ahead):
                    return table[ahead + jnp.maximum(count - j, 0)]

                shifts = (4, 2, 1, 7, 7)
            else:
                face, side, deep, edge, line = xl, yf, zf, el, ll

                def at(table, j, ahead):
                    return table[j - 1]

                shifts = (0, 0, 0, 0, 0)

            def pair(one, two):
                return jnp.where(half64, one, two).astype(BF16)

            f = [at(face, j, shifts[0]) for j in range(1, 5)]
            send[way, 0:64, :] = pair(f[0], f[1])
            send[way, 64:128, :] = pair(f[2], f[3])
            send[way, 128:192, :] = pair(at(side, 1, shifts[1]), at(side, 2, shifts[1]))
            d = at(deep, 1, shifts[2])
            send[way, 192:224, :] = jnp.where(half32, d[0:32], d[32:64]).astype(BF16)
            send[way, 320:384, :] = pair(f[0], f[1])
            for j in range(1, 7):
                e = at(edge, j, shifts[3])
                n = at(line, j, shifts[4])
                tile = jnp.concatenate(
                    [jnp.where(half8, e[0:8], n), jnp.where(half8, e[8:16], number)], axis=0
                ).astype(BF16)
                send[way, 224 + 16 * (j - 1) : 240 + 16 * (j - 1), :] = tile
                if j <= 5:
                    send[way, 384 + 16 * (j - 1) : 400 + 16 * (j - 1), :] = tile
                if j <= 3:
                    send[way, 464 + 16 * (j - 1) : 480 + 16 * (j - 1), :] = tile
                if j == 1:
                    send[way, 512:528, :] = tile

    def halo_copies(send, recv, ssem, rsem):
        copies = []
        for way, sign in ((0, 1), (1, -1)):
            for k in range(1, REACH + 1):
                rows = pl.ds(MSG_BASE[k - 1], MSG_ROWS[k - 1])
                copies.append(
                    pltpu.make_async_remote_copy(
                        src_ref=send.at[way, rows, :],
                        dst_ref=recv.at[way, rows, :],
                        send_sem=ssem.at[way, k - 1],
                        recv_sem=rsem.at[way, k - 1],
                        device_id=(jnp.clip(me + sign * k, 0, devices - 1),),
                        device_id_type=MESH,
                    )
                )
        return copies

    def each_sent(copies, act):
        for i, copy in enumerate(copies):
            sign = 1 if i < REACH else -1

            @pl.when(reached(sign, i % REACH + 1))
            def _():
                act(copy)

    def each_received(copies):
        for i, copy in enumerate(copies):
            sign = 1 if i < REACH else -1

            @pl.when(reached(-sign, i % REACH + 1))
            def _():
                copy.wait_recv()

    def unpack(recv):
        half64 = low_half((64, 128))
        half32 = low_half((32, 128))
        half16 = low_half((16, 128))

        def both(value, half):
            other = swap_halves(value)
            return jnp.where(half, value, other), jnp.where(half, other, value)

        for way in range(2):

            def rows(start, size):
                return recv[way, start : start + size, :].astype(F32)

            f1, f2 = both(rows(0, 64), half64)
            f3, f4 = both(rows(64, 64), half64)
            g1, g2 = both(rows(320, 64), half64)
            s1, s2 = both(rows(128, 64), half64)
            d1, d2 = both(rows(192, 32), half32)
            deep = jnp.concatenate([d1, d2], axis=0)
            tiles = {}
            starts = {1: (224, 6), 2: (384, 5), 3: (464, 3), 4: (512, 1)}
            for k, (start, many) in starts.items():
                for j in range(1, many + 1):
                    tiles[k, j] = both(rows(start + 16 * (j - 1), 16), half16)
            n1 = tiles[1, 1][1][8:16]
            c1 = n1
            c2 = c1 + tiles[2, 1][1][8:16]
            c3 = c2 + tiles[3, 1][1][8:16]

            def wide(mask):
                return jnp.concatenate([mask] * 8, axis=0)

            f3 = jnp.where(wide(c1 == 2.0), g1, f3)
            f4 = jnp.where(wide(c1 == 3.0), g1, jnp.where(wide(c1 == 2.0), g2, f4))
            edges, links = [], []
            for t in range(1, WIN + 1):
                e, n = tiles[1, t] if t <= 6 else tiles[4, 1]
                n = n[0:8]
                for j in range(1, 6):
                    if 2 <= t - j <= 6:
                        hit = c1 == float(t - j)
                        e2, n2 = tiles[2, j]
                        e = jnp.where(jnp.concatenate([hit, hit], axis=0), e2, e)
                        n = jnp.where(hit, n2[0:8], n)
                for j in range(1, 4):
                    if t - j >= 4:
                        hit = c2 == float(t - j)
                        e2, n2 = tiles[3, j]
                        e = jnp.where(jnp.concatenate([hit, hit], axis=0), e2, e)
                        n = jnp.where(hit, n2[0:8], n)
                if t == 7:
                    hit = c3 == 6.0
                    e2, n2 = tiles[4, 1]
                    e = jnp.where(jnp.concatenate([hit, hit], axis=0), e2, e)
                    n = jnp.where(hit, n2[0:8], n)
                edges.append(e)
                links.append(n)
            if way == 0:
                for t, f in enumerate((f1, f2, f3, f4), 1):
                    xh[4 - t] = f
                yb[1] = s1
                yb[0] = s2
                zb[0] = deep
                for t in range(1, WIN + 1):
                    eh[WIN - t] = edges[t - 1]
                    lh[WIN - t] = links[t - 1]
            else:
                for t, f in enumerate((f1, f2, f3, f4), 1):
                    xl[SLOTS - 1 + t] = f
                yf[SLOTS] = s1
                yf[SLOTS + 1] = s2
                zf[SLOTS] = deep
                for t in range(1, WIN + 1):
                    el[SLOTS - 1 + t] = edges[t - 1]
                    ll[SLOTS - 1 + t] = links[t - 1]

    def assemble(j):
        held, p, q, r = slot_facts(j)
        q1, r1 = q == 1, r == 1
        dz = jnp.where(r1, -1, 1)
        dy = jnp.where(q1, -2, 2)
        in_low = held & (p > 0)
        in_high = held & (p < last_section)
        zi = lax.broadcasted_iota(jnp.int32, (10, 8, 128), 1)
        bottom, top = zi == 0, zi == 7
        half = low_half((10, 8, 128))

        def put(x, center, side, deep, corner):
            none = jnp.zeros_like(side)
            ten = jnp.concatenate(
                [jnp.where(q1, side, none)[None], center, jnp.where(q1, none, side)[None]], axis=0
            )
            wide = jnp.broadcast_to(corner, (8, 128))
            inner = jnp.broadcast_to(deep[:, None, :], (8, 8, 128))
            row = jnp.concatenate(
                [jnp.where(q1, wide, none)[None], inner, jnp.where(q1, none, wide)[None]], axis=0
            )
            empty = jnp.zeros_like(row)
            before = jnp.where(bottom, jnp.where(r1, row, empty), pltpu.roll(ten, 1, 1))
            after = jnp.where(top, jnp.where(r1, empty, row), pltpu.roll(ten, 7, 1))
            near = jnp.where(half, before, ten)
            both = jnp.concatenate([near, after], axis=2).reshape(80, 256)
            padded[x, j] = both.astype(BF16)

        def gate(cond, value):
            return jnp.where(cond, value, jnp.zeros_like(value))

        low_at = j + 3
        corner_rows = eh[low_at + dy + dz]
        put(
            0,
            gate(in_low, xh[j]).reshape(8, 8, 128),
            gate(in_low, eh[low_at + dy][0:8]),
            gate(in_low, eh[low_at + dz][8:16]),
            gate(in_low, jnp.where(q1, corner_rows[15:16], corner_rows[8:9])),
        )
        corner_rows = el[forward_index(j + 4 + dy + dz)]
        put(
            9,
            gate(in_high, xl[jnp.minimum(forward_index(j + 4), 9)]).reshape(8, 8, 128),
            gate(in_high, el[forward_index(j + 4 + dy)][0:8]),
            gate(in_high, el[forward_index(j + 4 + dz)][8:16]),
            gate(in_high, jnp.where(q1, corner_rows[15:16], corner_rows[8:9])),
        )
        sides = gate(
            held, jnp.where(q1, yb[j], yf[jnp.minimum(forward_index(j + 2), SLOTS + 1)])
        )
        deeps = gate(held, jnp.where(r1, zb[j], zf[jnp.minimum(forward_index(j + 1), SLOTS)]))
        lines = gate(
            held,
            jnp.where(
                q1,
                lh[7 + j - jnp.where(r1, 3, 1)],
                ll[forward_index(j + jnp.where(r1, 1, 3))],
            ),
        )
        for x in range(8):
            rows = slice(x * 8, x * 8 + 8)
            put(
                x + 1,
                field[j, x * 64 : (x + 1) * 64, :].reshape(8, 8, 128),
                sides[rows],
                deeps[rows],
                lines[x : x + 1],
            )

    last_section = devices * 3 // 4 - 1

    def window(j, a):
        return padded[a : a + 8, j].reshape(640, 256)

    def combine(total):
        cube = total.reshape(8, 10, 8, 256)
        one = cube[:, 0:8, :, 0:128] + cube[:, 2:10, :, 128:256]
        two = swap_halves(cube[:, 1:9, :, 0:128].reshape(512, 128))
        return one.reshape(512, 128) + two

    fetches[0].wait()
    for j in range(SLOTS):
        value = vox_ref[j].astype(F32)
        field[j] = jnp.concatenate([value, value], axis=0).T
    for j in range(SLOTS):
        own_tables(j)

    pack(send1)
    chain = jnp.minimum(me, REACH) + jnp.minimum(devices - 1 - me, REACH)
    pl.semaphore_wait(barrier, chain + plane - 1 + planes - 1)
    first_copies = halo_copies(send1, recv1, ssem1, rsem1)
    each_sent(first_copies, lambda copy: copy.start())

    for fetch in fetches[1:]:
        fetch.wait()
    row_group = lax.broadcasted_iota(jnp.int32, (CH, 128), 0) // GC
    col_group = lax.rem(lanes((CH, 128)), CH) // GC
    same_group = row_group == col_group
    left = low_half((CH, 128))
    zero_half = jnp.zeros((GC, CH), F32)

    def spread(first_tap, second_tap):
        one = taps_ref[first_tap].astype(F32)
        two = zero_half if second_tap is None else taps_ref[second_tap].astype(F32)
        both = jnp.concatenate([one, two], axis=1)
        return jnp.where(same_group, jnp.concatenate([both] * GC, axis=0), 0.0).astype(BF16)

    blank = jnp.zeros((CH, 256), BF16)
    for a in range(3):
        for c in range(3):
            rows = slice(c * CH, (c + 1) * CH)
            weight_fwd[a, rows, 0:128] = spread(a * 9 + c, a * 9 + 3 + c)
            weight_fwd[a, rows, 128:256] = spread(a * 9 + 6 + c, None)
        weight_fwd[a, 3 * CH : 4 * CH, :] = blank
        for b in range(3):
            rows = slice(b * CH, (b + 1) * CH)
            base = (2 - a) * 9 + (2 - b) * 3
            weight_bwd[a, rows, 0:128] = spread(base + 2, base + 1)
            weight_bwd[a, rows, 128:256] = spread(base, None)
        weight_bwd[a, 3 * CH : 4 * CH, :] = blank

    bias_row = jnp.concatenate([bias_ref[...], bias_ref[...]], axis=1)

    each_received(first_copies)
    unpack(recv1)

    def forward(j):
        total = jnp.dot(window(j, 0), weight_fwd[0], preferred_element_type=F32)
        total += jnp.dot(window(j, 1), weight_fwd[1], preferred_element_type=F32)
        total += jnp.dot(window(j, 2), weight_fwd[2], preferred_element_type=F32)
        return combine(total) + bias_row

    def slopes(j):
        pre = pre_ref[j % 2].T[0:CH]
        held = brick_ref[j] >= 0
        keep = jnp.where(held, cortex_ref[j : j + 1, :], 0).astype(F32)
        sigma = jax.nn.sigmoid(pre)
        act_ref[j] = (pre * sigma * keep).astype(BF16)
        slope = sigma * (1.0 + pre * (1.0 - sigma))
        grad = (cot_ref[j].astype(F32) * keep * slope).astype(BF16).astype(F32)
        back = jnp.concatenate([grad, grad], axis=0).T
        field[j] = back
        cube = back.reshape(8, 8, 8, 128)
        gap = jnp.zeros((8, 1, 8, 128), F32)
        zero = jnp.concatenate([cube, gap, gap], axis=1)
        one = jnp.concatenate([gap, cube, gap], axis=1)
        two = jnp.concatenate([gap, gap, cube], axis=1)
        near = jnp.where(low_half((8, 10, 8, 128)), zero, one)
        shifted = jnp.concatenate([near, two], axis=3).reshape(8, 80, 256).astype(BF16)
        for x in range(8):
            spread_grad[j, x] = shifted[x]
        part_sum = jnp.sum(back.reshape(64, 8, 128), axis=0)
        bias_acc[...] = part_sum if j == 0 else bias_acc[...] + part_sum

    def kernel_terms(j):
        turned = spread_grad[j].reshape(640, 256).T
        for a in range(3):
            term = jnp.dot(turned, window(j, a), preferred_element_type=F32)
            acc[a] = term if j == 0 else acc[a] + term

    for step in range(SLOTS + 3):

        @pl.when(me >= 0)
        def _():
            if 0 <= step - 3:
                kernel_terms(step - 3)
            if 0 <= step - 2 < SLOTS:
                slopes(step - 2)
            if 0 <= step - 1 < SLOTS:
                pre_ref[(step - 1) % 2] = forward(step - 1)
            if step < SLOTS:
                assemble(step)

    lane_group = lax.rem(lanes((GC, 128)), CH) // GC
    half8 = low_half((GC, 128))
    tiles, halves = [], []
    for a in range(3):
        whole = acc[a].T
        for c in range(3):
            one = jnp.zeros((GC, 128), F32)
            two = jnp.zeros((GC, 128), F32)
            for g in range(8):
                rows = slice(c * CH + g * GC, c * CH + (g + 1) * GC)
                one = one + jnp.where(lane_group == g, whole[rows, 0:128], 0.0)
                two = two + jnp.where(lane_group == g, whole[rows, 128:256], 0.0)
            tiles.append(one)
            halves.append(two)
    halves.append(bias_acc[...])
    for i in range(5):
        tiles.append(jnp.where(half8, halves[2 * i], swap_halves(halves[2 * i + 1])))
    chunk = 128 // plane
    for i in range(16):
        tile = tiles[i] if i < 14 else jnp.zeros((GC, 128), F32)
        if chunk == 4:
            part[2 * i] = tile[0:4]
            part[2 * i + 1] = tile[4:8]
        else:
            per = chunk // 8
            part[i // per, (i % per) * 8 : (i % per) * 8 + 8, :] = tile

    def scatter_copy(i, many=1):
        to = lax.rem(mine + i, plane) if many == 1 else 0
        return pltpu.make_async_remote_copy(
            src_ref=part.at[pl.ds(to, many)],
            dst_ref=scattered.at[pl.ds(i, many)],
            send_sem=sems.at[0],
            recv_sem=sems.at[1],
            device_id=(plane_peer(i),),
            device_id_type=MESH,
        )

    def level_copy(i, many=1):
        return pltpu.make_async_remote_copy(
            src_ref=stacked.at[pl.ds(0, many)],
            dst_ref=stacked.at[pl.ds(i, many)],
            send_sem=sems.at[2],
            recv_sem=sems.at[3],
            device_id=(level_peer(i),),
            device_id_type=MESH,
        )

    def gather_copy(i, many=1):
        return pltpu.make_async_remote_copy(
            src_ref=final.at[pl.ds(0, many)],
            dst_ref=final.at[pl.ds(i, many)],
            send_sem=sems.at[4],
            recv_sem=sems.at[5],
            device_id=(plane_peer(i),),
            device_id_type=MESH,
        )

    def far_first(i, many):
        return lax.rem(i + many // 2, many - 1) + 1

    @pl.loop(0, plane - 1)
    def _(i):
        scatter_copy(far_first(i, plane)).start()

    scatter_copy(1, plane - 1).wait_recv()

    total = part[mine]
    for i in range(1, plane):
        total = total + scattered[i]
    stacked[0] = total

    @pl.loop(0, planes - 1)
    def _(i):
        level_copy(far_first(i, planes)).start()

    for j in range(SLOTS):
        own_tables(j)

    pack(send2)
    second_copies = halo_copies(send2, recv2, ssem2, rsem2)
    each_sent(second_copies, lambda copy: copy.start())

    each_received(second_copies)
    unpack(recv2)

    def input_gradient(j):
        assemble(j)
        dims = (((1,), (1,)), ((), ()))
        total = lax.dot_general(window(j, 0), weight_bwd[0], dims, preferred_element_type=F32)
        total += lax.dot_general(window(j, 1), weight_bwd[1], dims, preferred_element_type=F32)
        total += lax.dot_general(window(j, 2), weight_bwd[2], dims, preferred_element_type=F32)
        grad_ref[j] = combine(total).T[0:CH].astype(BF16)

    @pl.loop(0, SLOTS // 2)
    def _(j):
        input_gradient(j)

    level_copy(1, planes - 1).wait_recv()

    total = stacked[level]
    for i in range(1, planes):
        total = total + stacked[lax.rem(level + planes - i, planes)]
    final[0] = total

    @pl.loop(0, plane - 1)
    def _(i):
        gather_copy(far_first(i, plane)).start()

    @pl.loop(SLOTS // 2, SLOTS)
    def _(j):
        input_gradient(j)

    gather_copy(1, plane - 1).wait_recv()

    def gathered(m):
        return final[lax.rem(mine + plane - m, plane)]

    tiles = []
    for i in range(14):
        if chunk == 4:
            tiles.append(jnp.concatenate([gathered(2 * i), gathered(2 * i + 1)], axis=0))
        else:
            per = chunk // 8
            tiles.append(gathered(i // per)[(i % per) * 8 : (i % per) * 8 + 8])
    halves = []
    for i in range(5):
        halves.append(tiles[9 + i])
        halves.append(swap_halves(tiles[9 + i]))
    for a in range(3):
        for c in range(3):
            tile = tiles[a * 3 + c]
            kg_ref[a * 9 + c] = tile[:, 0:CH]
            kg_ref[a * 9 + 3 + c] = swap_halves(tile)[:, 0:CH]
            kg_ref[a * 9 + 6 + c] = halves[a * 3 + c][:, 0:CH]
    bg_ref[...] = jnp.sum(halves[9], axis=0, keepdims=True)[:, 0:CH]

    each_sent(first_copies, lambda copy: copy.wait_send())
    each_sent(second_copies, lambda copy: copy.wait_send())

    scatter_copy(1, plane - 1).wait_send()
    level_copy(1, planes - 1).wait_send()
    gather_copy(1, plane - 1).wait_send()


def copy_body(*refs):
    sources, targets, sem = refs[:4], refs[4:8], refs[8]
    copies = [
        pltpu.make_async_copy(source, target, sem.at[i])
        for i, (source, target) in enumerate(zip(sources, targets))
    ]
    for copy in copies:
        copy.start()
    for copy in copies:
        copy.wait()


def write_out(*values):
    return pl.pallas_call(
        copy_body,
        out_shape=tuple(jax.ShapeDtypeStruct(v.shape, v.dtype) for v in values),
        in_specs=[pl.BlockSpec(memory_space=pltpu.VMEM)] * 4,
        out_specs=(pl.BlockSpec(memory_space=pl.ANY),) * 4,
        scratch_shapes=[pltpu.SemaphoreType.DMA((4,))],
    )(*[pltpu.with_memory_space_constraint(v, pltpu.VMEM) for v in values])


def shards(devices, voxels, kernel, bias, cortex, slot_to_brick, neighbors, cotangent):
    plane = plane_size(devices)
    planes = devices // plane
    chunk = 128 // plane
    taps = jnp.transpose(kernel, (2, 3, 4, 1, 0)).reshape(27, GC, CH)
    vmem = pl.BlockSpec(memory_space=pltpu.VMEM)
    dma = pltpu.SemaphoreType.DMA
    act, grad, kg, bg = pl.pallas_call(
        functools.partial(kernel_body, devices, planes),
        out_shape=(
            pltpu.VMEM((SLOTS, CH, V), BF16),
            pltpu.VMEM((SLOTS, CH, V), BF16),
            pltpu.VMEM((27, GC, CH), F32),
            pltpu.VMEM((1, CH), F32),
        ),
        in_specs=[pl.BlockSpec(memory_space=pltpu.SMEM)]
        + [pl.BlockSpec(memory_space=pl.ANY)] * 5,
        out_specs=(vmem,) * 4,
        scratch_shapes=[
            pltpu.VMEM((SLOTS, CH, V), BF16),
            pltpu.VMEM((SLOTS, CH, V), BF16),
            pltpu.VMEM((SLOTS, V), jnp.int32),
            pltpu.VMEM((27, GC, CH), BF16),
            pltpu.VMEM((1, CH), F32),
            pltpu.VMEM((SLOTS, V, 128), F32),
            pltpu.VMEM((10, SLOTS, 80, 256), BF16),
            pltpu.VMEM((SLOTS, 8, 80, 256), BF16),
            pltpu.VMEM((2, V, 128), F32),
            pltpu.VMEM((3, 256, 256), F32),
            pltpu.VMEM((GC, 128), F32),
            pltpu.VMEM((3, 256, 256), BF16),
            pltpu.VMEM((3, 256, 256), BF16),
            pltpu.VMEM((10, 64, 128), F32),
            pltpu.VMEM((10, 64, 128), F32),
            pltpu.VMEM((8, 64, 128), F32),
            pltpu.VMEM((8, 64, 128), F32),
            pltpu.VMEM((7, 64, 128), F32),
            pltpu.VMEM((7, 64, 128), F32),
            pltpu.VMEM((13, 16, 128), F32),
            pltpu.VMEM((13, 16, 128), F32),
            pltpu.VMEM((13, 8, 128), F32),
            pltpu.VMEM((13, 8, 128), F32),
            pltpu.VMEM((2, MSG_TOTAL, 128), BF16),
            pltpu.VMEM((2, MSG_TOTAL, 128), BF16),
            pltpu.VMEM((2, MSG_TOTAL, 128), BF16),
            pltpu.VMEM((2, MSG_TOTAL, 128), BF16),
            pltpu.VMEM((plane, chunk, 128), F32),
            pltpu.VMEM((plane, chunk, 128), F32),
            pltpu.VMEM((planes, chunk, 128), F32),
            pltpu.VMEM((plane, chunk, 128), F32),
            dma((2, REACH)),
            dma((2, REACH)),
            dma((2, REACH)),
            dma((2, REACH)),
            dma((6,)),
            dma((5,)),
        ],
        compiler_params=pltpu.CompilerParams(
            collective_id=0, has_side_effects=True, vmem_limit_bytes=60 * 1024 * 1024
        ),
    )(slot_to_brick, voxels, cotangent, cortex, taps, bias.reshape(1, CH))
    act, grad, kg, bg = write_out(act, grad, kg, bg)
    kernel_grad = jnp.transpose(kg.reshape(3, 3, 3, GC, CH), (4, 3, 0, 1, 2))
    return (act, grad, kernel_grad, bg.reshape(CH))


def solution(mesh):
    devices = mesh.shape[AXIS]
    return jax.shard_map(
        functools.partial(shards, devices),
        mesh=mesh,
        in_specs=(
            P(AXIS, None, None),
            P(),
            P(),
            P(AXIS, None),
            P(AXIS),
            P(AXIS, None),
            P(AXIS, None, None),
        ),
        out_specs=(P(AXIS, None, None), P(AXIS, None, None), P(), P()),
        check_vma=False,
    )
```

```python
import functools

import jax
import jax.numpy as jnp
from jax import lax
from jax.experimental import pallas as pl
from jax.experimental.pallas import tpu as pltpu
from jax.sharding import PartitionSpec as P

AXIS = "bricks"
CH = 64
GC = 8
V = 512
SLOTS = 6
REACH = 4
WIN = 7
WIDE = 512
MSG_ROWS = (320, 144, 48, 16)
MSG_BASE = (0, 320, 464, 512)
MSG_TOTAL = 528
F32 = jnp.float32
BF16 = jnp.bfloat16
MESH = pl.DeviceIdType.MESH


def plane_size(devices):
    return 32 if devices >= 64 else devices // 2


def lanes(shape):
    return lax.broadcasted_iota(jnp.int32, shape, len(shape) - 1)


def low_half(shape):
    return lanes(shape) < CH


def swap_halves(value):
    return pltpu.roll(value, CH, value.ndim - 1)


def kernel_body(
    devices,
    planes,
    brick_ref,
    vox_hbm,
    cot_hbm,
    cortex_hbm,
    taps_hbm,
    bias_hbm,
    act_ref,
    grad_ref,
    kg_ref,
    bg_ref,
    vox_ref,
    cot_ref,
    cortex_ref,
    taps_ref,
    bias_ref,
    field,
    padded,
    spread_grad,
    pre_ref,
    turned,
    bias_acc,
    weight_fwd,
    weight_bwd,
    xh,
    xl,
    yb,
    yf,
    zb,
    zf,
    eh,
    el,
    lh,
    ll,
    send1,
    recv1,
    send2,
    recv2,
    part,
    scattered,
    stacked,
    final,
    ssem1,
    rsem1,
    ssem2,
    rsem2,
    sems,
    loads,
):
    plane = plane_size(devices)
    me = lax.axis_index(AXIS)
    mine = lax.rem(me, plane)
    level = me // plane

    def plane_peer(i):
        return level * plane + lax.rem(mine + i, plane)

    def level_peer(i):
        return lax.rem(level + i, planes) * plane + mine

    barrier = pltpu.get_barrier_semaphore()
    def reached(sign, k):
        return me + k < devices if sign > 0 else me >= k

    for k in range(1, REACH + 1):
        for sign in (-1, 1):

            @pl.when(reached(sign, k))
            def _():
                pl.semaphore_signal(
                    barrier, inc=1, device_id=(me + sign * k,), device_id_type=MESH
                )

    @pl.loop(1, plane)
    def _(i):
        pl.semaphore_signal(barrier, inc=1, device_id=(plane_peer(i),), device_id_type=MESH)

    @pl.loop(1, planes)
    def _(i):
        pl.semaphore_signal(barrier, inc=1, device_id=(level_peer(i),), device_id_type=MESH)

    fetches = [
        pltpu.make_async_copy(source, target, loads.at[i])
        for i, (source, target) in enumerate(
            (
                (vox_hbm, vox_ref),
                (taps_hbm, taps_ref),
                (cot_hbm, cot_ref),
                (cortex_hbm, cortex_ref),
                (bias_hbm, bias_ref),
            )
        )
    ]
    for fetch in fetches:
        fetch.start()

    count = jnp.int32(0)
    for j in range(SLOTS):
        count = count + jnp.where(brick_ref[j] >= 0, 1, 0).astype(jnp.int32)

    def forward_index(m):
        return jnp.minimum(jnp.where(m < count, m, SLOTS + m - count), 12)

    def slot_facts(j):
        brick = brick_ref[j]
        held = brick >= 0
        safe = jnp.maximum(brick, 0)
        return held, safe // 4, lax.rem(safe // 2, 2), lax.rem(safe, 2)

    def own_tables(j):
        held, _, q, r = slot_facts(j)
        q0, r0 = q == 0, r == 0
        high = field[j, 448:512, :]
        low = field[j, 0:64, :]
        xh[j + 4] = high
        xl[j] = low
        cube = field[j].reshape(8, 8, 8, 128)
        side = jnp.where(q0, cube[:, 7], cube[:, 0]).reshape(64, 128)
        yb[j + 2] = side
        yf[j] = side
        deep = jnp.where(
            r0, field[j, pl.ds(7, 64, stride=8), :], field[j, pl.ds(0, 64, stride=8), :]
        )
        zb[j + 1] = deep
        zf[j] = deep
        for table, at, start in ((eh, j + 7, 448), (el, j, 0)):
            table[at, 0:8, :] = jnp.where(
                q0, field[j, start + 56 : start + 64, :], field[j, start : start + 8, :]
            )
            table[at, 8:16, :] = jnp.where(
                r0,
                field[j, pl.ds(start + 7, 8, stride=8), :],
                field[j, pl.ds(start, 8, stride=8), :],
            )
        line = jnp.where(
            q0,
            jnp.where(
                r0,
                field[j, pl.ds(63, 8, stride=64), :],
                field[j, pl.ds(56, 8, stride=64), :],
            ),
            jnp.where(
                r0,
                field[j, pl.ds(7, 8, stride=64), :],
                field[j, pl.ds(0, 8, stride=64), :],
            ),
        )
        lh[j + 7] = line
        ll[j] = line

    def pack(send):
        half64 = low_half((64, 128))
        half32 = low_half((32, 128))
        half8 = low_half((8, 128))
        number = jnp.zeros((8, 128), F32) + count.astype(F32)
        for way in range(2):
            if way == 0:
                face, side, deep, edge, line = xh, yb, zb, eh, lh

                def at(table, j, ahead):
                    return table[ahead + jnp.maximum(count - j, 0)]

                shifts = (4, 2, 1, 7, 7)
            else:
                face, side, deep, edge, line = xl, yf, zf, el, ll

                def at(table, j, ahead):
                    return table[j - 1]

                shifts = (0, 0, 0, 0, 0)

            def pair(one, two):
                return jnp.where(half64, one, two).astype(BF16)

            f = [at(face, j, shifts[0]) for j in range(1, 5)]
            send[way, 0:64, :] = pair(f[0], f[1])
            send[way, 64:128, :] = pair(f[2], f[3])
            send[way, 128:192, :] = pair(at(side, 1, shifts[1]), at(side, 2, shifts[1]))
            d = at(deep, 1, shifts[2])
            send[way, 192:224, :] = jnp.where(half32, d[0:32], d[32:64]).astype(BF16)
            send[way, 320:384, :] = pair(f[0], f[1])
            for j in range(1, 7):
                e = at(edge, j, shifts[3])
                n = at(line, j, shifts[4])
                tile = jnp.concatenate(
                    [jnp.where(half8, e[0:8], n), jnp.where(half8, e[8:16], number)], axis=0
                ).astype(BF16)
                send[way, 224 + 16 * (j - 1) : 240 + 16 * (j - 1), :] = tile
                if j <= 5:
                    send[way, 384 + 16 * (j - 1) : 400 + 16 * (j - 1), :] = tile
                if j <= 3:
                    send[way, 464 + 16 * (j - 1) : 480 + 16 * (j - 1), :] = tile
                if j == 1:
                    send[way, 512:528, :] = tile

    def halo_copies(send, recv, ssem, rsem):
        copies = []
        for way, sign in ((0, 1), (1, -1)):
            for k in range(1, REACH + 1):
                rows = pl.ds(MSG_BASE[k - 1], MSG_ROWS[k - 1])
                copies.append(
                    pltpu.make_async_remote_copy(
                        src_ref=send.at[way, rows, :],
                        dst_ref=recv.at[way, rows, :],
                        send_sem=ssem.at[way, k - 1],
                        recv_sem=rsem.at[way, k - 1],
                        device_id=(jnp.clip(me + sign * k, 0, devices - 1),),
                        device_id_type=MESH,
                    )
                )
        return copies

    def each_sent(copies, act):
        for i, copy in enumerate(copies):
            sign = 1 if i < REACH else -1

            @pl.when(reached(sign, i % REACH + 1))
            def _():
                act(copy)

    def each_received(copies):
        for i, copy in enumerate(copies):
            sign = 1 if i < REACH else -1

            @pl.when(reached(-sign, i % REACH + 1))
            def _():
                copy.wait_recv()

    def unpack(recv):
        half64 = low_half((64, 128))
        half32 = low_half((32, 128))
        half16 = low_half((16, 128))

        def both(value, half):
            other = swap_halves(value)
            return jnp.where(half, value, other), jnp.where(half, other, value)

        for way in range(2):

            def rows(start, size):
                return recv[way, start : start + size, :].astype(F32)

            f1, f2 = both(rows(0, 64), half64)
            f3, f4 = both(rows(64, 64), half64)
            g1, g2 = both(rows(320, 64), half64)
            s1, s2 = both(rows(128, 64), half64)
            d1, d2 = both(rows(192, 32), half32)
            deep = jnp.concatenate([d1, d2], axis=0)
            tiles = {}
            starts = {1: (224, 6), 2: (384, 5), 3: (464, 3), 4: (512, 1)}
            for k, (start, many) in starts.items():
                for j in range(1, many + 1):
                    tiles[k, j] = both(rows(start + 16 * (j - 1), 16), half16)
            n1 = tiles[1, 1][1][8:16]
            c1 = n1
            c2 = c1 + tiles[2, 1][1][8:16]
            c3 = c2 + tiles[3, 1][1][8:16]

            def wide(mask):
                return jnp.concatenate([mask] * 8, axis=0)

            f3 = jnp.where(wide(c1 == 2.0), g1, f3)
            f4 = jnp.where(wide(c1 == 3.0), g1, jnp.where(wide(c1 == 2.0), g2, f4))
            edges, links = [], []
            for t in range(1, WIN + 1):
                e, n = tiles[1, t] if t <= 6 else tiles[4, 1]
                n = n[0:8]
                for j in range(1, 6):
                    if 2 <= t - j <= 6:
                        hit = c1 == float(t - j)
                        e2, n2 = tiles[2, j]
                        e = jnp.where(jnp.concatenate([hit, hit], axis=0), e2, e)
                        n = jnp.where(hit, n2[0:8], n)
                for j in range(1, 4):
                    if t - j >= 4:
                        hit = c2 == float(t - j)
                        e2, n2 = tiles[3, j]
                        e = jnp.where(jnp.concatenate([hit, hit], axis=0), e2, e)
                        n = jnp.where(hit, n2[0:8], n)
                if t == 7:
                    hit = c3 == 6.0
                    e2, n2 = tiles[4, 1]
                    e = jnp.where(jnp.concatenate([hit, hit], axis=0), e2, e)
                    n = jnp.where(hit, n2[0:8], n)
                edges.append(e)
                links.append(n)
            if way == 0:
                for t, f in enumerate((f1, f2, f3, f4), 1):
                    xh[4 - t] = f
                yb[1] = s1
                yb[0] = s2
                zb[0] = deep
                for t in range(1, WIN + 1):
                    eh[WIN - t] = edges[t - 1]
                    lh[WIN - t] = links[t - 1]
            else:
                for t, f in enumerate((f1, f2, f3, f4), 1):
                    xl[SLOTS - 1 + t] = f
                yf[SLOTS] = s1
                yf[SLOTS + 1] = s2
                zf[SLOTS] = deep
                for t in range(1, WIN + 1):
                    el[SLOTS - 1 + t] = edges[t - 1]
                    ll[SLOTS - 1 + t] = links[t - 1]

    def assemble(j):
        held, p, q, r = slot_facts(j)
        q1, r1 = q == 1, r == 1
        dz = jnp.where(r1, -1, 1)
        dy = jnp.where(q1, -2, 2)
        in_low = held & (p > 0)
        in_high = held & (p < last_section)
        zi = lax.broadcasted_iota(jnp.int32, (10, 8, 128), 1)
        bottom, top = zi == 0, zi == 7
        half = low_half((10, 8, 128))

        def put(x, center, side, deep, corner):
            none = jnp.zeros_like(side)
            ten = jnp.concatenate(
                [jnp.where(q1, side, none)[None], center, jnp.where(q1, none, side)[None]], axis=0
            )
            wide = jnp.broadcast_to(corner, (8, 128))
            inner = jnp.broadcast_to(deep[:, None, :], (8, 8, 128))
            row = jnp.concatenate(
                [jnp.where(q1, wide, none)[None], inner, jnp.where(q1, none, wide)[None]], axis=0
            )
            empty = jnp.zeros_like(row)
            before = jnp.where(bottom, jnp.where(r1, row, empty), pltpu.roll(ten, 1, 1))
            after = jnp.where(top, jnp.where(r1, empty, row), pltpu.roll(ten, 7, 1))
            near = jnp.where(half, before, ten)
            both = jnp.concatenate([near, after], axis=2).reshape(80, 256)
            padded[x, pl.ds(pl.multiple_of(j * 80, 16), 80), :] = both.astype(BF16)

        def gate(cond, value):
            return jnp.where(cond, value, jnp.zeros_like(value))

        low_at = j + 3
        corner_rows = eh[low_at + dy + dz]
        put(
            0,
            gate(in_low, xh[j]).reshape(8, 8, 128),
            gate(in_low, eh[low_at + dy][0:8]),
            gate(in_low, eh[low_at + dz][8:16]),
            gate(in_low, jnp.where(q1, corner_rows[15:16], corner_rows[8:9])),
        )
        corner_rows = el[forward_index(j + 4 + dy + dz)]
        put(
            9,
            gate(in_high, xl[jnp.minimum(forward_index(j + 4), 9)]).reshape(8, 8, 128),
            gate(in_high, el[forward_index(j + 4 + dy)][0:8]),
            gate(in_high, el[forward_index(j + 4 + dz)][8:16]),
            gate(in_high, jnp.where(q1, corner_rows[15:16], corner_rows[8:9])),
        )
        sides = gate(
            held, jnp.where(q1, yb[j], yf[jnp.minimum(forward_index(j + 2), SLOTS + 1)])
        )
        deeps = gate(held, jnp.where(r1, zb[j], zf[jnp.minimum(forward_index(j + 1), SLOTS)]))
        lines = gate(
            held,
            jnp.where(
                q1,
                lh[7 + j - jnp.where(r1, 3, 1)],
                ll[forward_index(j + jnp.where(r1, 1, 3))],
            ),
        )
        for x in range(8):
            rows = slice(x * 8, x * 8 + 8)
            put(
                x + 1,
                field[j, x * 64 : (x + 1) * 64, :].reshape(8, 8, 128),
                sides[rows],
                deeps[rows],
                lines[x : x + 1],
            )

    last_section = devices * 3 // 4 - 1

    def window(j, a):
        return padded[a : a + 8, pl.ds(pl.multiple_of(j * 80, 16), 80), :].reshape(640, 256)

    def combine(total):
        cube = total.reshape(8, 10, 8, 256)
        one = cube[:, 0:8, :, 0:128] + cube[:, 2:10, :, 128:256]
        two = swap_halves(cube[:, 1:9, :, 0:128].reshape(512, 128))
        return one.reshape(512, 128) + two

    fetches[0].wait()
    for j in range(SLOTS):
        value = vox_ref[j].astype(F32)
        field[j] = jnp.concatenate([value, value], axis=0).T
    for j in range(SLOTS):
        own_tables(j)

    pack(send1)
    chain = jnp.minimum(me, REACH) + jnp.minimum(devices - 1 - me, REACH)
    pl.semaphore_wait(barrier, chain + plane - 1 + planes - 1)
    first_copies = halo_copies(send1, recv1, ssem1, rsem1)
    each_sent(first_copies, lambda copy: copy.start())

    for fetch in fetches[1:]:
        fetch.wait()
    row_group = lax.broadcasted_iota(jnp.int32, (CH, 128), 0) // GC
    col_group = lax.rem(lanes((CH, 128)), CH) // GC
    same_group = row_group == col_group
    left = low_half((CH, 128))
    zero_half = jnp.zeros((GC, CH), F32)

    def spread(first_tap, second_tap):
        one = taps_ref[first_tap].astype(F32)
        two = zero_half if second_tap is None else taps_ref[second_tap].astype(F32)
        both = jnp.concatenate([one, two], axis=1)
        return jnp.where(same_group, jnp.concatenate([both] * GC, axis=0), 0.0).astype(BF16)

    blank = jnp.zeros((CH, 256), BF16)
    for a in range(3):
        for c in range(3):
            rows = slice(c * CH, (c + 1) * CH)
            weight_fwd[a, rows, 0:128] = spread(a * 9 + c, a * 9 + 3 + c)
            weight_fwd[a, rows, 128:256] = spread(a * 9 + 6 + c, None)
        weight_fwd[a, 3 * CH : 4 * CH, :] = blank
        for b in range(3):
            rows = slice(b * CH, (b + 1) * CH)
            base = (2 - a) * 9 + (2 - b) * 3
            weight_bwd[a, rows, 0:128] = spread(base + 2, base + 1)
            weight_bwd[a, rows, 128:256] = spread(base, None)
        weight_bwd[a, 3 * CH : 4 * CH, :] = blank

    for x in range(10):
        padded[x, SLOTS * 80 : WIDE, :] = jnp.zeros((WIDE - SLOTS * 80, 256), BF16)
    for x in range(8):
        spread_grad[x, SLOTS * 80 : WIDE, :] = jnp.zeros((WIDE - SLOTS * 80, 256), BF16)
    bias_row = jnp.concatenate([bias_ref[...], bias_ref[...]], axis=1)

    each_received(first_copies)
    unpack(recv1)

    def forward(j):
        total = jnp.dot(window(j, 0), weight_fwd[0], preferred_element_type=F32)
        total += jnp.dot(window(j, 1), weight_fwd[1], preferred_element_type=F32)
        total += jnp.dot(window(j, 2), weight_fwd[2], preferred_element_type=F32)
        pre_ref[j] = combine(total) + bias_row

    def turn(x):
        value = padded[x].T
        for a in range(3):
            if 0 <= x - a < 8:
                turned[a * 256 : (a + 1) * 256, (x - a) * WIDE : (x - a + 1) * WIDE] = value

    def slopes(j):
        pre = pre_ref[j].T[0:CH]
        held = brick_ref[j] >= 0
        keep = jnp.where(held, cortex_ref[j : j + 1, :], 0).astype(F32)
        sigma = jax.nn.sigmoid(pre)
        act_ref[j] = (pre * sigma * keep).astype(BF16)
        slope = sigma * (1.0 + pre * (1.0 - sigma))
        grad = (cot_ref[j].astype(F32) * keep * slope).astype(BF16).astype(F32)
        back = jnp.concatenate([grad, grad], axis=0).T
        field[j] = back
        cube = back.reshape(8, 8, 8, 128)
        gap = jnp.zeros((8, 1, 8, 128), F32)
        zero = jnp.concatenate([cube, gap, gap], axis=1)
        one = jnp.concatenate([gap, cube, gap], axis=1)
        two = jnp.concatenate([gap, gap, cube], axis=1)
        near = jnp.where(low_half((8, 10, 8, 128)), zero, one)
        shifted = jnp.concatenate([near, two], axis=3).reshape(8, 80, 256).astype(BF16)
        for x in range(8):
            spread_grad[x, j * 80 : (j + 1) * 80, :] = shifted[x]
        part_sum = jnp.sum(back.reshape(64, 8, 128), axis=0)
        bias_acc[...] = part_sum if j == 0 else bias_acc[...] + part_sum

    for step in range(5):
        if 0 <= step - 2:
            slopes(2 * step - 4)
            slopes(2 * step - 3)
        if 0 <= step - 1 < 3:
            forward(2 * step - 2)
            forward(2 * step - 1)
        if step < 3:
            assemble(2 * step)
            assemble(2 * step + 1)
        if step == 3:
            for x in range(10):
                turn(x)
    def kernel_half(i):
        return jnp.dot(
            turned[:, i * 4 * WIDE : (i + 1) * 4 * WIDE],
            spread_grad[4 * i : 4 * i + 4].reshape(4 * WIDE, 256),
            preferred_element_type=F32,
        )

    acc = kernel_half(0) + kernel_half(1)

    lane_group = lax.rem(lanes((GC, 128)), CH) // GC
    half8 = low_half((GC, 128))
    tiles, halves = [], []
    for a in range(3):
        whole = acc[a * 256 : (a + 1) * 256]
        for c in range(3):
            one = jnp.zeros((GC, 128), F32)
            two = jnp.zeros((GC, 128), F32)
            for g in range(8):
                rows = slice(c * CH + g * GC, c * CH + (g + 1) * GC)
                one = one + jnp.where(lane_group == g, whole[rows, 0:128], 0.0)
                two = two + jnp.where(lane_group == g, whole[rows, 128:256], 0.0)
            tiles.append(one)
            halves.append(two)
    halves.append(bias_acc[...])
    for i in range(5):
        tiles.append(jnp.where(half8, halves[2 * i], swap_halves(halves[2 * i + 1])))
    chunk = 128 // plane
    for i in range(16):
        tile = tiles[i] if i < 14 else jnp.zeros((GC, 128), F32)
        if chunk == 4:
            part[2 * i] = tile[0:4]
            part[2 * i + 1] = tile[4:8]
        else:
            per = chunk // 8
            part[i // per, (i % per) * 8 : (i % per) * 8 + 8, :] = tile

    def scatter_copy(i, many=1):
        to = lax.rem(mine + i, plane) if many == 1 else 0
        return pltpu.make_async_remote_copy(
            src_ref=part.at[pl.ds(to, many)],
            dst_ref=scattered.at[pl.ds(i, many)],
            send_sem=sems.at[0],
            recv_sem=sems.at[1],
            device_id=(plane_peer(i),),
            device_id_type=MESH,
        )

    def level_copy(i, many=1):
        return pltpu.make_async_remote_copy(
            src_ref=stacked.at[pl.ds(0, many)],
            dst_ref=stacked.at[pl.ds(i, many)],
            send_sem=sems.at[2],
            recv_sem=sems.at[3],
            device_id=(level_peer(i),),
            device_id_type=MESH,
        )

    def gather_copy(i, many=1):
        return pltpu.make_async_remote_copy(
            src_ref=final.at[pl.ds(0, many)],
            dst_ref=final.at[pl.ds(i, many)],
            send_sem=sems.at[4],
            recv_sem=sems.at[5],
            device_id=(plane_peer(i),),
            device_id_type=MESH,
        )

    def far_first(i, many):
        return lax.rem(i + many // 2, many - 1) + 1

    @pl.loop(0, plane - 1)
    def _(i):
        scatter_copy(far_first(i, plane)).start()

    for j in range(SLOTS):
        own_tables(j)

    pack(send2)
    scatter_copy(1, plane - 1).wait_recv()

    total = part[mine]
    for i in range(1, plane):
        total = total + scattered[i]
    stacked[0] = total

    @pl.loop(0, planes - 1)
    def _(i):
        level_copy(far_first(i, planes)).start()

    second_copies = halo_copies(send2, recv2, ssem2, rsem2)
    each_sent(second_copies, lambda copy: copy.start())

    def input_gradient(j):
        assemble(j)
        dims = (((1,), (1,)), ((), ()))
        total = lax.dot_general(window(j, 0), weight_bwd[0], dims, preferred_element_type=F32)
        total += lax.dot_general(window(j, 1), weight_bwd[1], dims, preferred_element_type=F32)
        total += lax.dot_general(window(j, 2), weight_bwd[2], dims, preferred_element_type=F32)
        grad_ref[j] = combine(total).T[0:CH].astype(BF16)

    level_copy(1, planes - 1).wait_recv()

    total = stacked[level]
    for i in range(1, planes):
        total = total + stacked[lax.rem(level + planes - i, planes)]
    final[0] = total

    @pl.loop(0, plane - 1)
    def _(i):
        gather_copy(far_first(i, plane)).start()

    each_received(second_copies)
    unpack(recv2)

    @pl.loop(0, SLOTS // 2)
    def _(j):
        input_gradient(2 * j)
        input_gradient(2 * j + 1)

    gather_copy(1, plane - 1).wait_recv()

    def gathered(m):
        return final[lax.rem(mine + plane - m, plane)]

    tiles = []
    for i in range(14):
        if chunk == 4:
            tiles.append(jnp.concatenate([gathered(2 * i), gathered(2 * i + 1)], axis=0))
        else:
            per = chunk // 8
            tiles.append(gathered(i // per)[(i % per) * 8 : (i % per) * 8 + 8])
    halves = []
    for i in range(5):
        halves.append(tiles[9 + i])
        halves.append(swap_halves(tiles[9 + i]))
    for a in range(3):
        for c in range(3):
            tile = tiles[a * 3 + c]
            kg_ref[a * 9 + c] = tile[:, 0:CH]
            kg_ref[a * 9 + 3 + c] = swap_halves(tile)[:, 0:CH]
            kg_ref[a * 9 + 6 + c] = halves[a * 3 + c][:, 0:CH]
    bg_ref[...] = jnp.sum(halves[9], axis=0, keepdims=True)[:, 0:CH]

    each_sent(first_copies, lambda copy: copy.wait_send())
    each_sent(second_copies, lambda copy: copy.wait_send())

    scatter_copy(1, plane - 1).wait_send()
    level_copy(1, planes - 1).wait_send()
    gather_copy(1, plane - 1).wait_send()


def copy_body(*refs):
    sources, targets, sem = refs[:4], refs[4:8], refs[8]
    copies = [
        pltpu.make_async_copy(source, target, sem.at[i])
        for i, (source, target) in enumerate(zip(sources, targets))
    ]
    for copy in copies:
        copy.start()
    for copy in copies:
        copy.wait()


def write_out(*values):
    return pl.pallas_call(
        copy_body,
        out_shape=tuple(jax.ShapeDtypeStruct(v.shape, v.dtype) for v in values),
        in_specs=[pl.BlockSpec(memory_space=pltpu.VMEM)] * 4,
        out_specs=(pl.BlockSpec(memory_space=pl.ANY),) * 4,
        scratch_shapes=[pltpu.SemaphoreType.DMA((4,))],
    )(*[pltpu.with_memory_space_constraint(v, pltpu.VMEM) for v in values])


def shards(devices, voxels, kernel, bias, cortex, slot_to_brick, neighbors, cotangent):
    plane = plane_size(devices)
    planes = devices // plane
    chunk = 128 // plane
    taps = jnp.transpose(kernel, (2, 3, 4, 1, 0)).reshape(27, GC, CH)
    vmem = pl.BlockSpec(memory_space=pltpu.VMEM)
    dma = pltpu.SemaphoreType.DMA
    act, grad, kg, bg = pl.pallas_call(
        functools.partial(kernel_body, devices, planes),
        out_shape=(
            pltpu.VMEM((SLOTS, CH, V), BF16),
            pltpu.VMEM((SLOTS, CH, V), BF16),
            pltpu.VMEM((27, GC, CH), F32),
            pltpu.VMEM((1, CH), F32),
        ),
        in_specs=[pl.BlockSpec(memory_space=pltpu.SMEM)]
        + [pl.BlockSpec(memory_space=pl.ANY)] * 5,
        out_specs=(vmem,) * 4,
        scratch_shapes=[
            pltpu.VMEM((SLOTS, CH, V), BF16),
            pltpu.VMEM((SLOTS, CH, V), BF16),
            pltpu.VMEM((SLOTS, V), jnp.int32),
            pltpu.VMEM((27, GC, CH), BF16),
            pltpu.VMEM((1, CH), F32),
            pltpu.VMEM((SLOTS, V, 128), F32),
            pltpu.VMEM((10, WIDE, 256), BF16),
            pltpu.VMEM((8, WIDE, 256), BF16),
            pltpu.VMEM((SLOTS, V, 128), F32),
            pltpu.VMEM((3 * 256, 8 * WIDE), BF16),
            pltpu.VMEM((GC, 128), F32),
            pltpu.VMEM((3, 256, 256), BF16),
            pltpu.VMEM((3, 256, 256), BF16),
            pltpu.VMEM((10, 64, 128), F32),
            pltpu.VMEM((10, 64, 128), F32),
            pltpu.VMEM((8, 64, 128), F32),
            pltpu.VMEM((8, 64, 128), F32),
            pltpu.VMEM((7, 64, 128), F32),
            pltpu.VMEM((7, 64, 128), F32),
            pltpu.VMEM((13, 16, 128), F32),
            pltpu.VMEM((13, 16, 128), F32),
            pltpu.VMEM((13, 8, 128), F32),
            pltpu.VMEM((13, 8, 128), F32),
            pltpu.VMEM((2, MSG_TOTAL, 128), BF16),
            pltpu.VMEM((2, MSG_TOTAL, 128), BF16),
            pltpu.VMEM((2, MSG_TOTAL, 128), BF16),
            pltpu.VMEM((2, MSG_TOTAL, 128), BF16),
            pltpu.VMEM((plane, chunk, 128), F32),
            pltpu.VMEM((plane, chunk, 128), F32),
            pltpu.VMEM((planes, chunk, 128), F32),
            pltpu.VMEM((plane, chunk, 128), F32),
            dma((2, REACH)),
            dma((2, REACH)),
            dma((2, REACH)),
            dma((2, REACH)),
            dma((6,)),
            dma((5,)),
        ],
        compiler_params=pltpu.CompilerParams(
            collective_id=0, has_side_effects=True, vmem_limit_bytes=60 * 1024 * 1024
        ),
    )(slot_to_brick, voxels, cotangent, cortex, taps, bias.reshape(1, CH))
    act, grad, kg, bg = write_out(act, grad, kg, bg)
    kernel_grad = jnp.transpose(kg.reshape(3, 3, 3, GC, CH), (4, 3, 0, 1, 2))
    return (act, grad, kernel_grad, bg.reshape(CH))


def solution(mesh):
    devices = mesh.shape[AXIS]
    return jax.shard_map(
        functools.partial(shards, devices),
        mesh=mesh,
        in_specs=(
            P(AXIS, None, None),
            P(),
            P(),
            P(AXIS, None),
            P(AXIS),
            P(AXIS, None),
            P(AXIS, None, None),
        ),
        out_specs=(P(AXIS, None, None), P(AXIS, None, None), P(), P()),
        check_vma=False,
    )
```

```python
import functools

import jax
import jax.numpy as jnp
from jax import lax
from jax.experimental import pallas as pl
from jax.experimental.pallas import tpu as pltpu
from jax.sharding import PartitionSpec as P

AXIS = "bricks"
CH = 64
GC = 8
V = 512
SLOTS = 6
REACH = 4
WIN = 7
WIDE = 512
MSG_ROWS = (320, 144, 48, 16)
MSG_BASE = (0, 320, 464, 512)
MSG_TOTAL = 528
F32 = jnp.float32
BF16 = jnp.bfloat16
MESH = pl.DeviceIdType.MESH


def plane_size(devices):
    return 32 if devices >= 64 else devices // 2


def lanes(shape):
    return lax.broadcasted_iota(jnp.int32, shape, len(shape) - 1)


def low_half(shape):
    return lanes(shape) < CH


def swap_halves(value):
    return pltpu.roll(value, CH, value.ndim - 1)


def kernel_body(
    devices,
    planes,
    brick_ref,
    vox_hbm,
    cot_hbm,
    cortex_hbm,
    taps_hbm,
    bias_hbm,
    act_ref,
    grad_ref,
    kg_ref,
    bg_ref,
    vox_ref,
    cot_ref,
    cortex_ref,
    taps_ref,
    bias_ref,
    field,
    padded,
    spread_grad,
    pre_ref,
    turned,
    own_part,
    bias_acc,
    weight_fwd,
    weight_bwd,
    xh,
    xl,
    yb,
    yf,
    zb,
    zf,
    eh,
    el,
    lh,
    ll,
    send1,
    recv1,
    send2,
    recv2,
    part,
    scattered,
    stacked,
    final,
    ssem1,
    rsem1,
    ssem2,
    rsem2,
    sems,
    loads,
):
    plane = plane_size(devices)
    me = lax.axis_index(AXIS)
    mine = lax.rem(me, plane)
    level = me // plane

    def plane_peer(i):
        return level * plane + lax.rem(mine + i, plane)

    def level_peer(i):
        return lax.rem(level + i, planes) * plane + mine

    barrier = pltpu.get_barrier_semaphore()
    def reached(sign, k):
        return me + k < devices if sign > 0 else me >= k

    for k in range(1, REACH + 1):
        for sign in (-1, 1):

            @pl.when(reached(sign, k))
            def _():
                pl.semaphore_signal(
                    barrier, inc=1, device_id=(me + sign * k,), device_id_type=MESH
                )

    @pl.loop(1, plane)
    def _(i):
        pl.semaphore_signal(barrier, inc=1, device_id=(plane_peer(i),), device_id_type=MESH)

    @pl.loop(1, planes)
    def _(i):
        pl.semaphore_signal(barrier, inc=1, device_id=(level_peer(i),), device_id_type=MESH)

    fetches = [
        pltpu.make_async_copy(source, target, loads.at[i])
        for i, (source, target) in enumerate(
            (
                (vox_hbm, vox_ref),
                (taps_hbm, taps_ref),
                (cot_hbm, cot_ref),
                (cortex_hbm, cortex_ref),
                (bias_hbm, bias_ref),
            )
        )
    ]
    for fetch in fetches:
        fetch.start()

    count = jnp.int32(0)
    for j in range(SLOTS):
        count = count + jnp.where(brick_ref[j] >= 0, 1, 0).astype(jnp.int32)

    def forward_index(m):
        return jnp.minimum(jnp.where(m < count, m, SLOTS + m - count), 12)

    def slot_facts(j):
        brick = brick_ref[j]
        held = brick >= 0
        safe = jnp.maximum(brick, 0)
        return held, safe // 4, lax.rem(safe // 2, 2), lax.rem(safe, 2)

    def own_tables(j):
        held, _, q, r = slot_facts(j)
        q0, r0 = q == 0, r == 0
        high = field[j, 448:512, :]
        low = field[j, 0:64, :]
        xh[j + 4] = high
        xl[j] = low
        cube = field[j].reshape(8, 8, 8, 128)
        side = jnp.where(q0, cube[:, 7], cube[:, 0]).reshape(64, 128)
        yb[j + 2] = side
        yf[j] = side
        deep = jnp.where(
            r0, field[j, pl.ds(7, 64, stride=8), :], field[j, pl.ds(0, 64, stride=8), :]
        )
        zb[j + 1] = deep
        zf[j] = deep
        for table, at, start in ((eh, j + 7, 448), (el, j, 0)):
            table[at, 0:8, :] = jnp.where(
                q0, field[j, start + 56 : start + 64, :], field[j, start : start + 8, :]
            )
            table[at, 8:16, :] = jnp.where(
                r0,
                field[j, pl.ds(start + 7, 8, stride=8), :],
                field[j, pl.ds(start, 8, stride=8), :],
            )
        line = jnp.where(
            q0,
            jnp.where(
                r0,
                field[j, pl.ds(63, 8, stride=64), :],
                field[j, pl.ds(56, 8, stride=64), :],
            ),
            jnp.where(
                r0,
                field[j, pl.ds(7, 8, stride=64), :],
                field[j, pl.ds(0, 8, stride=64), :],
            ),
        )
        lh[j + 7] = line
        ll[j] = line

    def pack(send):
        half64 = low_half((64, 128))
        half32 = low_half((32, 128))
        half8 = low_half((8, 128))
        number = jnp.zeros((8, 128), F32) + count.astype(F32)
        for way in range(2):
            if way == 0:
                face, side, deep, edge, line = xh, yb, zb, eh, lh

                def at(table, j, ahead):
                    return table[ahead + jnp.maximum(count - j, 0)]

                shifts = (4, 2, 1, 7, 7)
            else:
                face, side, deep, edge, line = xl, yf, zf, el, ll

                def at(table, j, ahead):
                    return table[j - 1]

                shifts = (0, 0, 0, 0, 0)

            def pair(one, two):
                return jnp.where(half64, one, two).astype(BF16)

            f = [at(face, j, shifts[0]) for j in range(1, 5)]
            send[way, 0:64, :] = pair(f[0], f[1])
            send[way, 64:128, :] = pair(f[2], f[3])
            send[way, 128:192, :] = pair(at(side, 1, shifts[1]), at(side, 2, shifts[1]))
            d = at(deep, 1, shifts[2])
            send[way, 192:224, :] = jnp.where(half32, d[0:32], d[32:64]).astype(BF16)
            send[way, 320:384, :] = pair(f[0], f[1])
            for j in range(1, 7):
                e = at(edge, j, shifts[3])
                n = at(line, j, shifts[4])
                tile = jnp.concatenate(
                    [jnp.where(half8, e[0:8], n), jnp.where(half8, e[8:16], number)], axis=0
                ).astype(BF16)
                send[way, 224 + 16 * (j - 1) : 240 + 16 * (j - 1), :] = tile
                if j <= 5:
                    send[way, 384 + 16 * (j - 1) : 400 + 16 * (j - 1), :] = tile
                if j <= 3:
                    send[way, 464 + 16 * (j - 1) : 480 + 16 * (j - 1), :] = tile
                if j == 1:
                    send[way, 512:528, :] = tile

    def halo_copies(send, recv, ssem, rsem):
        copies = []
        for way, sign in ((0, 1), (1, -1)):
            for k in range(1, REACH + 1):
                rows = pl.ds(MSG_BASE[k - 1], MSG_ROWS[k - 1])
                copies.append(
                    pltpu.make_async_remote_copy(
                        src_ref=send.at[way, rows, :],
                        dst_ref=recv.at[way, rows, :],
                        send_sem=ssem.at[way, k - 1],
                        recv_sem=rsem.at[way, k - 1],
                        device_id=(jnp.clip(me + sign * k, 0, devices - 1),),
                        device_id_type=MESH,
                    )
                )
        return copies

    def each_sent(copies, act):
        for i, copy in enumerate(copies):
            sign = 1 if i < REACH else -1

            @pl.when(reached(sign, i % REACH + 1))
            def _():
                act(copy)

    def each_received(copies):
        for i, copy in enumerate(copies):
            sign = 1 if i < REACH else -1

            @pl.when(reached(-sign, i % REACH + 1))
            def _():
                copy.wait_recv()

    def unpack(recv):
        half64 = low_half((64, 128))
        half32 = low_half((32, 128))
        half16 = low_half((16, 128))

        def both(value, half):
            other = swap_halves(value)
            return jnp.where(half, value, other), jnp.where(half, other, value)

        for way in range(2):

            def rows(start, size):
                return recv[way, start : start + size, :].astype(F32)

            f1, f2 = both(rows(0, 64), half64)
            f3, f4 = both(rows(64, 64), half64)
            g1, g2 = both(rows(320, 64), half64)
            s1, s2 = both(rows(128, 64), half64)
            d1, d2 = both(rows(192, 32), half32)
            deep = jnp.concatenate([d1, d2], axis=0)
            tiles = {}
            starts = {1: (224, 6), 2: (384, 5), 3: (464, 3), 4: (512, 1)}
            for k, (start, many) in starts.items():
                for j in range(1, many + 1):
                    tiles[k, j] = both(rows(start + 16 * (j - 1), 16), half16)
            n1 = tiles[1, 1][1][8:16]
            c1 = n1
            c2 = c1 + tiles[2, 1][1][8:16]
            c3 = c2 + tiles[3, 1][1][8:16]

            def wide(mask):
                return jnp.concatenate([mask] * 8, axis=0)

            f3 = jnp.where(wide(c1 == 2.0), g1, f3)
            f4 = jnp.where(wide(c1 == 3.0), g1, jnp.where(wide(c1 == 2.0), g2, f4))
            edges, links = [], []
            for t in range(1, WIN + 1):
                e, n = tiles[1, t] if t <= 6 else tiles[4, 1]
                n = n[0:8]
                for j in range(1, 6):
                    if 2 <= t - j <= 6:
                        hit = c1 == float(t - j)
                        e2, n2 = tiles[2, j]
                        e = jnp.where(jnp.concatenate([hit, hit], axis=0), e2, e)
                        n = jnp.where(hit, n2[0:8], n)
                for j in range(1, 4):
                    if t - j >= 4:
                        hit = c2 == float(t - j)
                        e2, n2 = tiles[3, j]
                        e = jnp.where(jnp.concatenate([hit, hit], axis=0), e2, e)
                        n = jnp.where(hit, n2[0:8], n)
                if t == 7:
                    hit = c3 == 6.0
                    e2, n2 = tiles[4, 1]
                    e = jnp.where(jnp.concatenate([hit, hit], axis=0), e2, e)
                    n = jnp.where(hit, n2[0:8], n)
                edges.append(e)
                links.append(n)
            if way == 0:
                for t, f in enumerate((f1, f2, f3, f4), 1):
                    xh[4 - t] = f
                yb[1] = s1
                yb[0] = s2
                zb[0] = deep
                for t in range(1, WIN + 1):
                    eh[WIN - t] = edges[t - 1]
                    lh[WIN - t] = links[t - 1]
            else:
                for t, f in enumerate((f1, f2, f3, f4), 1):
                    xl[SLOTS - 1 + t] = f
                yf[SLOTS] = s1
                yf[SLOTS + 1] = s2
                zf[SLOTS] = deep
                for t in range(1, WIN + 1):
                    el[SLOTS - 1 + t] = edges[t - 1]
                    ll[SLOTS - 1 + t] = links[t - 1]

    def assemble(j, ready=False):
        held, p, q, r = slot_facts(j)
        q1, r1 = q == 1, r == 1
        dz = jnp.where(r1, -1, 1)
        dy = jnp.where(q1, -2, 2)
        in_low = held & (p > 0)
        in_high = held & (p < last_section)
        zi = lax.broadcasted_iota(jnp.int32, (10, 8, 128), 1)
        bottom, top = zi == 0, zi == 7
        half = low_half((10, 8, 128))

        def put(x, center, side, deep, corner):
            none = jnp.zeros_like(side)
            ten = jnp.concatenate(
                [jnp.where(q1, side, none)[None], center, jnp.where(q1, none, side)[None]], axis=0
            )
            wide = jnp.broadcast_to(corner, (8, 128))
            inner = jnp.broadcast_to(deep[:, None, :], (8, 8, 128))
            row = jnp.concatenate(
                [jnp.where(q1, wide, none)[None], inner, jnp.where(q1, none, wide)[None]], axis=0
            )
            empty = jnp.zeros_like(row)
            before = jnp.where(bottom, jnp.where(r1, row, empty), pltpu.roll(ten, 1, 1))
            after = jnp.where(top, jnp.where(r1, empty, row), pltpu.roll(ten, 7, 1))
            near = jnp.where(half, before, ten)
            both = jnp.concatenate([near, after], axis=2).reshape(80, 256)
            padded[x, pl.ds(pl.multiple_of(j * 80, 16), 80), :] = both.astype(BF16)

        def put_ready(x, side, deep, corner):
            none = jnp.zeros_like(side)
            wide = jnp.broadcast_to(corner, (8, 128))
            first = jnp.where(q1, wide, none)
            last = jnp.where(q1, none, wide)
            ends = jnp.concatenate(
                [jnp.where(q1, side, none)[None], jnp.where(q1, none, side)[None]], axis=0
            )
            edge = jnp.concatenate([first[None], last[None]], axis=0)
            inner = jnp.broadcast_to(deep[:, None, :], (8, 8, 128))
            blank = jnp.zeros_like(edge)
            before = jnp.where(
                bottom[0:2], jnp.where(r1, edge, blank), pltpu.roll(ends, 1, 1)
            )
            after = jnp.where(top[0:2], jnp.where(r1, blank, edge), pltpu.roll(ends, 7, 1))
            near = jnp.where(half[0:2], before, ends)
            own_near = jnp.where(
                jnp.logical_and(jnp.logical_and(bottom, half)[0:8], r1),
                inner,
                own_part[j, x - 1, :, :, 0:128],
            )
            own_after = jnp.where(
                jnp.logical_and(top[0:8], jnp.logical_not(r1)),
                inner,
                own_part[j, x - 1, :, :, 128:256],
            )
            near = jnp.concatenate([near[0:1], own_near, near[1:2]], axis=0)
            after = jnp.concatenate([after[0:1], own_after, after[1:2]], axis=0)
            both = jnp.concatenate([near, after], axis=2).reshape(80, 256)
            padded[x, pl.ds(pl.multiple_of(j * 80, 16), 80), :] = both.astype(BF16)

        def gate(cond, value):
            return jnp.where(cond, value, jnp.zeros_like(value))

        low_at = j + 3
        corner_rows = eh[low_at + dy + dz]
        put(
            0,
            gate(in_low, xh[j]).reshape(8, 8, 128),
            gate(in_low, eh[low_at + dy][0:8]),
            gate(in_low, eh[low_at + dz][8:16]),
            gate(in_low, jnp.where(q1, corner_rows[15:16], corner_rows[8:9])),
        )
        corner_rows = el[forward_index(j + 4 + dy + dz)]
        put(
            9,
            gate(in_high, xl[jnp.minimum(forward_index(j + 4), 9)]).reshape(8, 8, 128),
            gate(in_high, el[forward_index(j + 4 + dy)][0:8]),
            gate(in_high, el[forward_index(j + 4 + dz)][8:16]),
            gate(in_high, jnp.where(q1, corner_rows[15:16], corner_rows[8:9])),
        )
        sides = gate(
            held, jnp.where(q1, yb[j], yf[jnp.minimum(forward_index(j + 2), SLOTS + 1)])
        )
        deeps = gate(held, jnp.where(r1, zb[j], zf[jnp.minimum(forward_index(j + 1), SLOTS)]))
        lines = gate(
            held,
            jnp.where(
                q1,
                lh[7 + j - jnp.where(r1, 3, 1)],
                ll[forward_index(j + jnp.where(r1, 1, 3))],
            ),
        )
        for x in range(8):
            rows = slice(x * 8, x * 8 + 8)
            if ready:
                put_ready(x + 1, sides[rows], deeps[rows], lines[x : x + 1])
                continue
            put(
                x + 1,
                field[j, x * 64 : (x + 1) * 64, :].reshape(8, 8, 128),
                sides[rows],
                deeps[rows],
                lines[x : x + 1],
            )

    def prepare(j):
        zi = lax.broadcasted_iota(jnp.int32, (8, 8, 128), 1)
        half = low_half((8, 8, 128))
        for x in range(8):
            center = field[j, x * 64 : (x + 1) * 64, :].reshape(8, 8, 128)
            blank = jnp.zeros_like(center)
            before = jnp.where(zi == 0, blank, pltpu.roll(center, 1, 1))
            own_part[j, x, :, :, 0:128] = jnp.where(half, before, center)
            own_part[j, x, :, :, 128:256] = jnp.where(zi == 7, blank, pltpu.roll(center, 7, 1))

    last_section = devices * 3 // 4 - 1

    def window(j, a):
        return padded[a : a + 8, pl.ds(pl.multiple_of(j * 80, 16), 80), :].reshape(640, 256)

    def combine(total):
        cube = total.reshape(8, 10, 8, 256)
        one = cube[:, 0:8, :, 0:128] + cube[:, 2:10, :, 128:256]
        two = swap_halves(cube[:, 1:9, :, 0:128].reshape(512, 128))
        return one.reshape(512, 128) + two

    fetches[0].wait()
    for j in range(SLOTS):
        value = vox_ref[j].astype(F32)
        field[j] = jnp.concatenate([value, value], axis=0).T
    for j in range(SLOTS):
        own_tables(j)

    pack(send1)
    chain = jnp.minimum(me, REACH) + jnp.minimum(devices - 1 - me, REACH)
    pl.semaphore_wait(barrier, chain + plane - 1 + planes - 1)
    first_copies = halo_copies(send1, recv1, ssem1, rsem1)
    each_sent(first_copies, lambda copy: copy.start())

    for fetch in fetches[1:]:
        fetch.wait()
    row_group = lax.broadcasted_iota(jnp.int32, (CH, 128), 0) // GC
    col_group = lax.rem(lanes((CH, 128)), CH) // GC
    same_group = row_group == col_group
    left = low_half((CH, 128))
    zero_half = jnp.zeros((GC, CH), F32)

    def spread(first_tap, second_tap):
        one = taps_ref[first_tap].astype(F32)
        two = zero_half if second_tap is None else taps_ref[second_tap].astype(F32)
        both = jnp.concatenate([one, two], axis=1)
        return jnp.where(same_group, jnp.concatenate([both] * GC, axis=0), 0.0).astype(BF16)

    blank = jnp.zeros((CH, 256), BF16)
    for a in range(3):
        for c in range(3):
            rows = slice(c * CH, (c + 1) * CH)
            weight_fwd[a, rows, 0:128] = spread(a * 9 + c, a * 9 + 3 + c)
            weight_fwd[a, rows, 128:256] = spread(a * 9 + 6 + c, None)
        weight_fwd[a, 3 * CH : 4 * CH, :] = blank
        for b in range(3):
            rows = slice(b * CH, (b + 1) * CH)
            base = (2 - a) * 9 + (2 - b) * 3
            weight_bwd[a, rows, 0:128] = spread(base + 2, base + 1)
            weight_bwd[a, rows, 128:256] = spread(base, None)
        weight_bwd[a, 3 * CH : 4 * CH, :] = blank

    for x in range(10):
        padded[x, SLOTS * 80 : WIDE, :] = jnp.zeros((WIDE - SLOTS * 80, 256), BF16)
    for x in range(8):
        spread_grad[x, SLOTS * 80 : WIDE, :] = jnp.zeros((WIDE - SLOTS * 80, 256), BF16)
    for j in range(SLOTS):
        prepare(j)
    bias_row = jnp.concatenate([bias_ref[...], bias_ref[...]], axis=1)

    each_received(first_copies)
    unpack(recv1)

    def forward(j):
        total = jnp.dot(window(j, 0), weight_fwd[0], preferred_element_type=F32)
        total += jnp.dot(window(j, 1), weight_fwd[1], preferred_element_type=F32)
        total += jnp.dot(window(j, 2), weight_fwd[2], preferred_element_type=F32)
        pre_ref[j] = combine(total) + bias_row

    def turn(x):
        value = padded[x].T
        for a in range(3):
            if 0 <= x - a < 8:
                turned[a * 256 : (a + 1) * 256, (x - a) * WIDE : (x - a + 1) * WIDE] = value

    def slopes(j):
        pre = pre_ref[j].T[0:CH]
        held = brick_ref[j] >= 0
        keep = jnp.where(held, cortex_ref[j : j + 1, :], 0).astype(F32)
        sigma = jax.nn.sigmoid(pre)
        act_ref[j] = (pre * sigma * keep).astype(BF16)
        slope = sigma * (1.0 + pre * (1.0 - sigma))
        grad = (cot_ref[j].astype(F32) * keep * slope).astype(BF16).astype(F32)
        back = jnp.concatenate([grad, grad], axis=0).T
        field[j] = back
        cube = back.reshape(8, 8, 8, 128)
        gap = jnp.zeros((8, 1, 8, 128), F32)
        zero = jnp.concatenate([cube, gap, gap], axis=1)
        one = jnp.concatenate([gap, cube, gap], axis=1)
        two = jnp.concatenate([gap, gap, cube], axis=1)
        near = jnp.where(low_half((8, 10, 8, 128)), zero, one)
        shifted = jnp.concatenate([near, two], axis=3).reshape(8, 80, 256).astype(BF16)
        for x in range(8):
            spread_grad[x, j * 80 : (j + 1) * 80, :] = shifted[x]
        part_sum = jnp.sum(back.reshape(64, 8, 128), axis=0)
        bias_acc[...] = part_sum if j == 0 else bias_acc[...] + part_sum

    for step in range(5):
        if 0 <= step - 2:
            slopes(2 * step - 4)
            slopes(2 * step - 3)
        if 0 <= step - 1 < 3:
            forward(2 * step - 2)
            forward(2 * step - 1)
        if step < 3:
            assemble(2 * step, True)
            assemble(2 * step + 1, True)
        if step == 3:
            for x in range(10):
                turn(x)
    def kernel_half(i):
        return jnp.dot(
            turned[:, i * 2 * WIDE : (i + 1) * 2 * WIDE],
            spread_grad[2 * i : 2 * i + 2].reshape(2 * WIDE, 256),
            preferred_element_type=F32,
        )

    acc = (kernel_half(0) + kernel_half(1)) + (kernel_half(2) + kernel_half(3))

    lane_group = lax.rem(lanes((GC, 128)), CH) // GC
    half8 = low_half((GC, 128))
    tiles, halves = [], []
    for a in range(3):
        whole = acc[a * 256 : (a + 1) * 256]
        for c in range(3):
            one = jnp.zeros((GC, 128), F32)
            two = jnp.zeros((GC, 128), F32)
            for g in range(8):
                rows = slice(c * CH + g * GC, c * CH + (g + 1) * GC)
                one = one + jnp.where(lane_group == g, whole[rows, 0:128], 0.0)
                two = two + jnp.where(lane_group == g, whole[rows, 128:256], 0.0)
            tiles.append(one)
            halves.append(two)
    halves.append(bias_acc[...])
    for i in range(5):
        tiles.append(jnp.where(half8, halves[2 * i], swap_halves(halves[2 * i + 1])))
    chunk = 128 // plane
    for i in range(16):
        tile = tiles[i] if i < 14 else jnp.zeros((GC, 128), F32)
        if chunk == 4:
            part[2 * i] = tile[0:4]
            part[2 * i + 1] = tile[4:8]
        else:
            per = chunk // 8
            part[i // per, (i % per) * 8 : (i % per) * 8 + 8, :] = tile

    def scatter_copy(i, many=1):
        to = lax.rem(mine + i, plane) if many == 1 else 0
        return pltpu.make_async_remote_copy(
            src_ref=part.at[pl.ds(to, many)],
            dst_ref=scattered.at[pl.ds(i, many)],
            send_sem=sems.at[0],
            recv_sem=sems.at[1],
            device_id=(plane_peer(i),),
            device_id_type=MESH,
        )

    def level_copy(i, many=1):
        return pltpu.make_async_remote_copy(
            src_ref=stacked.at[pl.ds(0, many)],
            dst_ref=stacked.at[pl.ds(i, many)],
            send_sem=sems.at[2],
            recv_sem=sems.at[3],
            device_id=(level_peer(i),),
            device_id_type=MESH,
        )

    def gather_copy(i, many=1):
        return pltpu.make_async_remote_copy(
            src_ref=final.at[pl.ds(0, many)],
            dst_ref=final.at[pl.ds(i, many)],
            send_sem=sems.at[4],
            recv_sem=sems.at[5],
            device_id=(plane_peer(i),),
            device_id_type=MESH,
        )

    def far_first(i, many):
        return lax.rem(i + many // 2, many - 1) + 1

    @pl.loop(0, plane - 1)
    def _(i):
        scatter_copy(far_first(i, plane)).start()

    for j in range(SLOTS):
        own_tables(j)

    pack(send2)
    scatter_copy(1, plane - 1).wait_recv()

    total = part[mine]
    for i in range(1, plane):
        total = total + scattered[i]
    stacked[0] = total

    @pl.loop(0, planes - 1)
    def _(i):
        level_copy(far_first(i, planes)).start()

    second_copies = halo_copies(send2, recv2, ssem2, rsem2)
    each_sent(second_copies, lambda copy: copy.start())

    def input_gradient(j):
        assemble(j)
        dims = (((1,), (1,)), ((), ()))
        total = lax.dot_general(window(j, 0), weight_bwd[0], dims, preferred_element_type=F32)
        total += lax.dot_general(window(j, 1), weight_bwd[1], dims, preferred_element_type=F32)
        total += lax.dot_general(window(j, 2), weight_bwd[2], dims, preferred_element_type=F32)
        grad_ref[j] = combine(total).T[0:CH].astype(BF16)

    level_copy(1, planes - 1).wait_recv()

    total = stacked[level]
    for i in range(1, planes):
        total = total + stacked[lax.rem(level + planes - i, planes)]
    final[0] = total

    @pl.loop(0, plane - 1)
    def _(i):
        gather_copy(far_first(i, plane)).start()

    each_received(second_copies)
    unpack(recv2)

    @pl.loop(0, SLOTS // 2)
    def _(j):
        input_gradient(2 * j)
        input_gradient(2 * j + 1)

    gather_copy(1, plane - 1).wait_recv()

    def gathered(m):
        return final[lax.rem(mine + plane - m, plane)]

    tiles = []
    for i in range(14):
        if chunk == 4:
            tiles.append(jnp.concatenate([gathered(2 * i), gathered(2 * i + 1)], axis=0))
        else:
            per = chunk // 8
            tiles.append(gathered(i // per)[(i % per) * 8 : (i % per) * 8 + 8])
    halves = []
    for i in range(5):
        halves.append(tiles[9 + i])
        halves.append(swap_halves(tiles[9 + i]))
    for a in range(3):
        for c in range(3):
            tile = tiles[a * 3 + c]
            kg_ref[a * 9 + c] = tile[:, 0:CH]
            kg_ref[a * 9 + 3 + c] = swap_halves(tile)[:, 0:CH]
            kg_ref[a * 9 + 6 + c] = halves[a * 3 + c][:, 0:CH]
    bg_ref[...] = jnp.sum(halves[9], axis=0, keepdims=True)[:, 0:CH]

    each_sent(first_copies, lambda copy: copy.wait_send())
    each_sent(second_copies, lambda copy: copy.wait_send())

    scatter_copy(1, plane - 1).wait_send()
    level_copy(1, planes - 1).wait_send()
    gather_copy(1, plane - 1).wait_send()


def copy_body(*refs):
    sources, targets, sem = refs[:4], refs[4:8], refs[8]
    copies = [
        pltpu.make_async_copy(source, target, sem.at[i])
        for i, (source, target) in enumerate(zip(sources, targets))
    ]
    for copy in copies:
        copy.start()
    for copy in copies:
        copy.wait()


def write_out(*values):
    return pl.pallas_call(
        copy_body,
        out_shape=tuple(jax.ShapeDtypeStruct(v.shape, v.dtype) for v in values),
        in_specs=[pl.BlockSpec(memory_space=pltpu.VMEM)] * 4,
        out_specs=(pl.BlockSpec(memory_space=pl.ANY),) * 4,
        scratch_shapes=[pltpu.SemaphoreType.DMA((4,))],
    )(*[pltpu.with_memory_space_constraint(v, pltpu.VMEM) for v in values])


def shards(devices, voxels, kernel, bias, cortex, slot_to_brick, neighbors, cotangent):
    plane = plane_size(devices)
    planes = devices // plane
    chunk = 128 // plane
    taps = jnp.transpose(kernel, (2, 3, 4, 1, 0)).reshape(27, GC, CH)
    vmem = pl.BlockSpec(memory_space=pltpu.VMEM)
    dma = pltpu.SemaphoreType.DMA
    act, grad, kg, bg = pl.pallas_call(
        functools.partial(kernel_body, devices, planes),
        out_shape=(
            pltpu.VMEM((SLOTS, CH, V), BF16),
            pltpu.VMEM((SLOTS, CH, V), BF16),
            pltpu.VMEM((27, GC, CH), F32),
            pltpu.VMEM((1, CH), F32),
        ),
        in_specs=[pl.BlockSpec(memory_space=pltpu.SMEM)]
        + [pl.BlockSpec(memory_space=pl.ANY)] * 5,
        out_specs=(vmem,) * 4,
        scratch_shapes=[
            pltpu.VMEM((SLOTS, CH, V), BF16),
            pltpu.VMEM((SLOTS, CH, V), BF16),
            pltpu.VMEM((SLOTS, V), jnp.int32),
            pltpu.VMEM((27, GC, CH), BF16),
            pltpu.VMEM((1, CH), F32),
            pltpu.VMEM((SLOTS, V, 128), F32),
            pltpu.VMEM((10, WIDE, 256), BF16),
            pltpu.VMEM((8, WIDE, 256), BF16),
            pltpu.VMEM((SLOTS, V, 128), F32),
            pltpu.VMEM((3 * 256, 8 * WIDE), BF16),
            pltpu.VMEM((SLOTS, 8, 8, 8, 256), F32),
            pltpu.VMEM((GC, 128), F32),
            pltpu.VMEM((3, 256, 256), BF16),
            pltpu.VMEM((3, 256, 256), BF16),
            pltpu.VMEM((10, 64, 128), F32),
            pltpu.VMEM((10, 64, 128), F32),
            pltpu.VMEM((8, 64, 128), F32),
            pltpu.VMEM((8, 64, 128), F32),
            pltpu.VMEM((7, 64, 128), F32),
            pltpu.VMEM((7, 64, 128), F32),
            pltpu.VMEM((13, 16, 128), F32),
            pltpu.VMEM((13, 16, 128), F32),
            pltpu.VMEM((13, 8, 128), F32),
            pltpu.VMEM((13, 8, 128), F32),
            pltpu.VMEM((2, MSG_TOTAL, 128), BF16),
            pltpu.VMEM((2, MSG_TOTAL, 128), BF16),
            pltpu.VMEM((2, MSG_TOTAL, 128), BF16),
            pltpu.VMEM((2, MSG_TOTAL, 128), BF16),
            pltpu.VMEM((plane, chunk, 128), F32),
            pltpu.VMEM((plane, chunk, 128), F32),
            pltpu.VMEM((planes, chunk, 128), F32),
            pltpu.VMEM((plane, chunk, 128), F32),
            dma((2, REACH)),
            dma((2, REACH)),
            dma((2, REACH)),
            dma((2, REACH)),
            dma((6,)),
            dma((5,)),
        ],
        compiler_params=pltpu.CompilerParams(
            collective_id=0, has_side_effects=True, vmem_limit_bytes=60 * 1024 * 1024
        ),
    )(slot_to_brick, voxels, cotangent, cortex, taps, bias.reshape(1, CH))
    act, grad, kg, bg = write_out(act, grad, kg, bg)
    kernel_grad = jnp.transpose(kg.reshape(3, 3, 3, GC, CH), (4, 3, 0, 1, 2))
    return (act, grad, kernel_grad, bg.reshape(CH))


def solution(mesh):
    devices = mesh.shape[AXIS]
    return jax.shard_map(
        functools.partial(shards, devices),
        mesh=mesh,
        in_specs=(
            P(AXIS, None, None),
            P(),
            P(),
            P(AXIS, None),
            P(AXIS),
            P(AXIS, None),
            P(AXIS, None, None),
        ),
        out_specs=(P(AXIS, None, None), P(AXIS, None, None), P(), P()),
        check_vma=False,
    )
```
